128 devices in a mesh: wide: 16 (over z_hi, x, core), narrow: 8 (over y, z_lo).
Axes of the slice: x: 4, y: 4, z: 4 (z_hi: 2, z_lo: 2; z = z_hi * 2 + z_lo), core: 2. Of those that a mesh axis runs over, the one named last changes fastest.
Arguments:
- hidden: bfloat16 [4096, 14336], P('narrow', 'wide'), may hold values from -6 to 6
- out_grad: bfloat16 [4096, 4096], P('wide', 'narrow'), may hold values from -6 to 6
- sign_bits: int32 [14336, 4096], P('wide', 'narrow'), may hold values 0 or 1
- pick_rows: int32 [8192], replicated, may hold values from 0 to 14335
- pick_cols: int32 [8192], replicated, may hold values from 0 to 4095
Outputs:
- sketch: float32 [2, 8192], replicated
The draws below stay inside these ranges and needn't reach their ends.
All inputs are finite; a program needn't handle non-finite values. No bound on the sum of `sign_bits` on one device may be relied on, other than what follows from the above.
Results may differ from the reference program's by a relative error of at most 0.0003.
Values may be sent and summed in bfloat16 or wider, within the bound.
A program may use at most 64 MiB of HBM per device.

```python
import math
import jax
import jax.numpy as jnp

D = 4096
FF = 14336
EXAMPLES = 2
SEQ = 2048
GROUPS = 16
BAND = 128
SKETCH = 8192
TOKENS = 4096


def place_ends(result, rng, low, high):
    longest = result.shape.index(max(result.shape))
    spots = []
    for shift in (0, 1):
        where = [jax.random.randint(jax.random.fold_in(rng, axis), (), 0, length) for axis, length in enumerate(result.shape)]
        where[longest] = (where[longest] + shift) % result.shape[longest]
        spots.append(tuple(where))
    return result.at[spots[0]].set(low).at[spots[1]].set(high)


def level_of(rng, dims, shards, smallest, largest):
    def one(axis_at, shards_of):
        steps = jax.random.uniform(jax.random.fold_in(jax.random.fold_in(rng, 6), axis_at), (shards_of,), jnp.float32, smallest / len(shards), largest / len(shards))
        return jnp.repeat(jnp.exp(steps), dims[axis_at] // shards_of).reshape((-1,) + (1,) * (len(dims) - axis_at - 1))

    factor_of = one(*shards[0])
    for cut in shards[1:]:
        factor_of = factor_of * one(*cut)
    return factor_of


def centred(own_key, shape, scale, most, cuts=(), kind=jnp.bfloat16):
    gain = level_of(own_key, shape, cuts, -0.22, 0.18) if cuts else 1.0
    entries = jax.random.normal(own_key, shape, jnp.float32) * scale * gain
    return jnp.minimum(jnp.maximum(entries, -most), most).astype(kind)


def setup_inputs(seed: int = 0) -> dict:
    seeds = jax.random.split(jax.random.key(seed), 6)
    return {
        "hidden": centred(seeds[0], (TOKENS, FF), 1.0, 6.0, ((0, 8), (1, 16))),
        "out_grad": centred(seeds[1], (TOKENS, D), 1.0, 6.0, ((0, 16), (1, 8))),
        "sign_bits": place_ends((jax.random.randint(seeds[2], (FF, D), 0, 2) < 1).astype(jnp.int32), jax.random.fold_in(seeds[2], 1), 0, 1),
        "pick_rows": place_ends(jax.random.randint(seeds[3], (SKETCH,), 0, FF), jax.random.fold_in(seeds[3], 1), 0, FF - 1).astype(jnp.int32),
        "pick_cols": place_ends(jax.random.randint(seeds[4], (SKETCH,), 0, D), jax.random.fold_in(seeds[4], 1), 0, D - 1).astype(jnp.int32),
    }


def walsh_last(values):
    length = values.shape[-1]
    leading = values.shape[:-1]
    stride = 1
    while stride < length:
        pieces = values.reshape(leading + (length // (2 * stride), 2, stride))
        upper_half = pieces[..., 0, :]
        lower_half = pieces[..., 1, :]
        values = jnp.stack([upper_half + lower_half, upper_half - lower_half], axis=-2).reshape(leading + (length,))
        stride = stride * 2
    return values

def reference(hidden, out_grad, sign_bits, pick_rows, pick_cols):
    flips = (2 * sign_bits - 1).astype(jnp.float32)
    middle = FF // (GROUPS * BAND)
    factor = 1.0 / math.sqrt(GROUPS * BAND * D * SEQ)
    results = []
    for example in range(EXAMPLES):
        activations = hidden[example * SEQ:(example + 1) * SEQ]
        gradients = out_grad[example * SEQ:(example + 1) * SEQ]
        gradient = jnp.dot(activations.T, gradients, preferred_element_type=jnp.float32)
        flipped = gradient * flips
        columns = walsh_last(flipped)
        blocks = columns.reshape(GROUPS, middle, BAND, D)
        blocks = jnp.moveaxis(walsh_last(jnp.moveaxis(blocks, 0, -1)), -1, 0)
        blocks = jnp.moveaxis(walsh_last(jnp.moveaxis(blocks, 2, -1)), -1, 2)
        whole = blocks.reshape(FF, D)
        results.append(whole[pick_rows, pick_cols] * factor)
    return jnp.stack(results)
```

```python
import math

import jax
import jax.numpy as jnp
from jax import lax
from jax.sharding import PartitionSpec as P

EXAMPLES = 2
SEQ = 2048
GROUPS = 16
BAND = 128


def bit_parity(value, count):
    total = jnp.zeros_like(value)
    for bit_num in range(count):
        total = total + jnp.bitwise_and(jnp.right_shift(value, bit_num), 1)
    return total % 2


def walsh_table(length):
    numbers = lax.iota(jnp.int32, length)
    parity = bit_parity(
        jnp.bitwise_and(numbers[:, None], numbers[None, :]), length.bit_length() - 1
    )
    return (1 - 2 * parity).astype(jnp.float32) / math.sqrt(length)


def shards(hidden, out_grad, sign_bits, pick_rows, pick_cols):
    acts_all = lax.all_gather(hidden, "narrow", axis=0, tiled=True)
    grads_all = lax.all_gather(out_grad, "wide", axis=0, tiled=True)
    rows_local = acts_all.shape[1]
    cols_local = grads_all.shape[1]
    acts_all = acts_all.reshape(EXAMPLES, -1, rows_local)
    grads_all = grads_all.reshape(EXAMPLES, -1, cols_local)
    gradient = jnp.einsum("esr,esc->erc", acts_all, grads_all, preferred_element_type=jnp.float32)
    flipped = gradient * (2 * sign_bits - 1).astype(jnp.float32)[None]
    wide_count = lax.axis_size("wide")
    narrow_count = lax.axis_size("narrow")
    groups_local = GROUPS // wide_count
    middle = rows_local // (groups_local * BAND)
    blocks = flipped.reshape(EXAMPLES, groups_local, middle, BAND, cols_local)
    blocks = jnp.einsum(
        "ehmpc,gh->egmpc", blocks, walsh_table(groups_local), precision=lax.Precision.HIGHEST
    )
    blocks = jnp.einsum(
        "ehmpc,qp->ehmqc", blocks, walsh_table(BAND), precision=lax.Precision.HIGHEST
    )
    blocks = jnp.dot(
        blocks.reshape(-1, cols_local), walsh_table(cols_local), precision=lax.Precision.HIGHEST
    )
    local = blocks.reshape(EXAMPLES, rows_local * cols_local)
    position = pick_rows % rows_local * cols_local + pick_cols % cols_local
    row_owner = pick_rows // rows_local
    col_owner = pick_cols // cols_local
    wide_index = lax.axis_index("wide")
    narrow_index = lax.axis_index("narrow")
    picked = local[:, position]
    flips = bit_parity(
        jnp.bitwise_and(row_owner, wide_index), wide_count.bit_length() - 1
    ) + bit_parity(jnp.bitwise_and(col_owner, narrow_index), narrow_count.bit_length() - 1)
    scale = 1.0 / math.sqrt(SEQ * wide_count * narrow_count)
    terms = picked * ((1 - 2 * (flips % 2)).astype(jnp.float32) * scale)[None, :]
    return lax.psum(terms, ("wide", "narrow"))


def solution(mesh):
    placed = (P("narrow", "wide"), P("wide", "narrow"), P("wide", "narrow"), P(), P())
    return jax.shard_map(shards, mesh=mesh, in_specs=placed, out_specs=P(), check_vma=False)
```

```python
import math

import jax
import jax.numpy as jnp
from jax import lax
from jax.experimental import pallas as pl
from jax.experimental.pallas import tpu as pltpu
from jax.sharding import PartitionSpec as P

SEQ = 2048
BAND = 128
LANES = 128
WIDE = 16
NARROW = 8
MESH = pl.DeviceIdType.MESH


def bit_parity(value, count):
    total = jnp.zeros_like(value)
    for bit_num in range(count):
        total = total + jnp.bitwise_and(jnp.right_shift(value, bit_num), 1)
    return jnp.bitwise_and(total, 1)


def place():
    wide, narrow = lax.axis_index("wide"), lax.axis_index("narrow")
    return wide // 8, (wide // 2) % 4, wide % 2, narrow // 2, narrow % 2


def device(z_hi, x, core, y, z_lo):
    return (z_hi * 8 + x * 2 + core, y * 2 + z_lo)


def transform_kernel(
    acts, grads, signs, out, hbuf, gbuf, sbuf, total,
    local_sem, hy_send, hz_send, h_recv, init_send, x_send, relay_send, g_recv,
    core_send, core_recv, s_send, s_recv,
):
    z_hi, x, core, y, z_lo = place()
    y_pair = y + 1 - 2 * (y % 2)
    at_y = device(z_hi, x, core, y_pair, z_lo)
    at_z = device(z_hi, x, core, y, 1 - z_lo)
    at_far = device(z_hi, x, core, 3 - y, z_lo)
    at_hi = device(1 - z_hi, x, core, y, z_lo)
    at_hi_far = device(1 - z_hi, x, core, 3 - y, z_lo)
    at_right = device(z_hi, (x + 1) % 4, core, y, z_lo)
    at_left = device(z_hi, (x + 3) % 4, core, y, z_lo)
    at_core = device(z_hi, x, 1 - core, y, z_lo)
    peers = (at_y, at_z, at_far, at_hi, at_hi_far, at_right, at_left, at_core)
    holder = y // 2 == z_hi
    chunk = acts.shape[0] // 4

    barrier = pltpu.get_barrier_semaphore()
    for peer in peers:
        pl.semaphore_signal(barrier, inc=1, device_id=peer, device_id_type=MESH)
    pl.semaphore_wait(barrier, len(peers))

    def remote(src, dst, send, recv, target):
        return pltpu.make_async_remote_copy(
            src_ref=src, dst_ref=dst, send_sem=send, recv_sem=recv, device_id=target, device_id_type=MESH
        )

    def arrived(ref, recv):
        remote(ref, ref, s_send, recv, at_core).wait_recv()

    own_h = pltpu.make_async_copy(acts, hbuf.at[0], local_sem.at[0])
    own_s = pltpu.make_async_copy(signs, sbuf.at[0], local_sem.at[1])
    own_g = pltpu.make_async_copy(grads, gbuf.at[0, core, 0], local_sem.at[2])
    to_hi = remote(grads, gbuf.at[0, core, 0], init_send.at[0], g_recv.at[0, 0], at_hi)
    to_far = remote(grads, gbuf.at[0, core, 1], init_send.at[0], g_recv.at[0, 1], at_far)
    to_hi_far = remote(grads, gbuf.at[0, core, 1], init_send.at[1], g_recv.at[0, 1], at_hi_far)

    @pl.when(holder)
    def _():
        own_g.start()
        to_hi.start()

    @pl.when(jnp.logical_not(holder))
    def _():
        to_far.start()
        to_hi_far.start()

    pending = []
    for first, second in zip((0, 1, 2, 3), (2, 3, 0, 1)):
        for num, slot, sends, target in ((first, 1, hy_send, at_y), (second, 2, hz_send, at_z)):
            copy = remote(
                acts.at[pl.ds(num * chunk, chunk)], hbuf.at[slot, pl.ds(num * chunk, chunk)],
                sends.at[num], h_recv.at[slot - 1, num], target,
            )
            copy.start()
            pending.append(copy)
    send_s = remote(signs, sbuf.at[1], s_send, s_recv, at_far)
    send_s.start()
    own_h.start()
    own_s.start()

    def rows(slot, num):
        return hbuf.at[slot, pl.ds(num * chunk, chunk)]

    def pass_on(slot, num):
        arrived(rows(slot, num), h_recv.at[slot - 1, num])
        sends, target = ((hz_send, at_z), (hy_send, at_y))[slot - 1]
        copy = remote(rows(slot, num), rows(3, num), sends.at[4 + num % 2], h_recv.at[2, num], target)
        copy.start()
        pending.append(copy)

    def to_sibling(slot, part):
        block = gbuf.at[slot, core, part]
        copy = remote(block, block, core_send.at[slot, part], core_recv.at[slot, part], at_core)
        copy.start()
        pending.append(copy)

    def spread(part):
        block = gbuf.at[0, core, part]
        for side, target in ((1, at_right), (2, at_left)):
            copy = remote(
                block, gbuf.at[side, core, part], x_send.at[side - 1, part], g_recv.at[side, part], target
            )
            copy.start()
            pending.append(copy)
        to_sibling(0, part)

    def around(part):
        for side in (1, 2):
            arrived(gbuf.at[side, core, part], g_recv.at[side, part])
        for side, target in ((1, at_right), (2, at_left)):

            @pl.when(core == side - 1)
            def _():
                remote(
                    gbuf.at[side, core, part], gbuf.at[3, core, part],
                    relay_send.at[part], g_recv.at[3, part], target,
                ).start()

        to_sibling(1, part)
        to_sibling(2, part)

    @pl.when(holder)
    def _():
        own_g.wait()

    @pl.when(jnp.logical_not(holder))
    def _():
        arrived(gbuf.at[0, core, 0], g_recv.at[0, 0])

    spread(0)
    pass_on(1, 0)
    pass_on(2, 2)
    arrived(gbuf.at[0, core, 1], g_recv.at[0, 1])
    spread(1)
    pass_on(1, 1)
    pass_on(2, 3)
    around(0)
    around(1)
    for part in range(2):
        arrived(gbuf.at[3, core, part], g_recv.at[3, part])
        to_sibling(3, part)

    total[...] = jnp.zeros_like(total)
    own_h.wait()
    for slot in range(4):
        for part in range(2):
            arrived(gbuf.at[slot, 1 - core, part], core_recv.at[slot, part])

    y_bit, depth = y % 2, acts.shape[0] // 2

    def step(num, carry):
        slot, half = num // 2, num % 2
        for at, which, nums in ((3, 1, (2, 3)), (4, 2, (0, 1)), (6, 3, (0, 1)), (7, 3, (2, 3))):

            @pl.when(num == at)
            def _():
                for one in nums:
                    arrived(rows(which, one), h_recv.at[which - 1, one])

        from_y, from_z = slot % 2, slot // 2
        tokens = ((y_bit + from_y) % 2) * 2 + (z_lo + from_z) % 2
        ahead = (tokens - x + 4) % 4
        source = (ahead + (ahead + 1) // 2) % 4
        left = hbuf[slot, pl.ds(pl.multiple_of(half * depth, depth), depth), :]
        for part in range(2):
            total[part] += lax.dot_general(
                left, gbuf[source, half, part], (((0,), (0,)), ((), ())), preferred_element_type=jnp.float32
            )
        return carry

    lax.fori_loop(0, 8, step, 0)
    own_s.wait()
    arrived(sbuf.at[1], s_recv)

    row_nums = lax.broadcasted_iota(jnp.int32, (BAND, BAND), 0)
    col_nums = lax.broadcasted_iota(jnp.int32, (BAND, BAND), 1)
    walsh = (1 - 2 * bit_parity(jnp.bitwise_and(row_nums, col_nums), 7)).astype(jnp.float32).astype(jnp.bfloat16)

    def mix(group, carry):
        band = pl.ds(pl.multiple_of(group * BAND, BAND), BAND)
        values = []
        for part in range(2):
            flipped = total[part, band, :] * sbuf[part, band, :].astype(jnp.float32)
            high = flipped.astype(jnp.bfloat16)
            low = (flipped - high.astype(jnp.float32)).astype(jnp.bfloat16)
            mixed = jnp.dot(walsh, high, preferred_element_type=jnp.float32)
            mixed = mixed + jnp.dot(walsh, low, preferred_element_type=jnp.float32)
            values += [mixed[:, k * LANES:(k + 1) * LANES] for k in range(4)]
        for stride in (1, 2, 4):
            values = [
                values[k - stride] - values[k] if k & stride else values[k] + values[k + stride]
                for k in range(8)
            ]
        for k in range(8):
            out[k, band, :] = values[k]
        return carry

    lax.fori_loop(0, total.shape[1] // BAND, mix, 0)

    for copy in pending:
        copy.wait_send()
    send_s.wait_send()
    for part in range(2):
        remote(
            gbuf.at[1, core, part], gbuf.at[3, core, part], relay_send.at[part], g_recv.at[3, part], at_core
        ).wait_send()
    to_hi.wait_send()

    @pl.when(jnp.logical_not(holder))
    def _():
        to_hi_far.wait_send()


def transform(hidden, out_grad, signs):
    tokens, units = hidden.shape
    part_tokens, features = out_grad.shape
    dma = pltpu.SemaphoreType.DMA
    return pl.pallas_call(
        transform_kernel,
        out_shape=jax.ShapeDtypeStruct((8, units, LANES), jnp.float32),
        in_specs=[pl.BlockSpec(memory_space=pl.ANY)] * 3,
        out_specs=pl.BlockSpec(memory_space=pltpu.VMEM),
        scratch_shapes=[
            pltpu.VMEM((4, tokens, units), jnp.bfloat16),
            pltpu.VMEM((4, 2, 2, part_tokens, features), jnp.bfloat16),
            pltpu.VMEM((2, units, features), jnp.bfloat16),
            pltpu.VMEM((2, units, features), jnp.float32),
            dma((3,)), dma((6,)), dma((6,)), dma((3, 4)), dma((2,)), dma((2, 2)), dma((2,)), dma((4, 2)),
            dma((4, 2)), dma((4, 2)), dma, dma,
        ],
        compiler_params=pltpu.CompilerParams(
            collective_id=0, has_side_effects=True, vmem_limit_bytes=48 * 1024 * 1024
        ),
        name="gather_transform",
    )(hidden, out_grad, signs)


def pick_kernel(spots, table, weights, out):
    lane_nums = lax.broadcasted_iota(jnp.int32, (8, LANES), 1)
    sub_nums = lax.broadcasted_iota(jnp.int32, (8, LANES), 0)
    unroll = 8

    for tile in range(8):

        def step(block, found):
            for inner in range(unroll):
                lane = block * unroll + inner
                rows = jnp.zeros((8, LANES), jnp.float32)
                for sub in range(8):
                    spot = spots[tile * 1024 + sub * LANES + lane]
                    row = jnp.broadcast_to(table[pl.ds(spot, 1), :], (8, LANES))
                    rows = row if sub == 0 else jnp.where(sub_nums == sub, row, rows)
                at = pl.multiple_of((tile * LANES + lane) * 8, 8)
                value = jnp.sum(rows * weights[pl.ds(at, 8), :], axis=1, keepdims=True)
                found = jnp.where(lane_nums == lane, value, found)
            return found

        found = lax.fori_loop(0, LANES // unroll, step, jnp.zeros((8, LANES), jnp.float32))
        out[2 * tile] = found[:4]
        out[2 * tile + 1] = found[4:]


def pick(spots, table, weights):
    return pl.pallas_call(
        pick_kernel,
        out_shape=jax.ShapeDtypeStruct((WIDE, 4, LANES), jnp.float32),
        in_specs=[
            pl.BlockSpec(memory_space=pltpu.SMEM),
            pl.BlockSpec(memory_space=pltpu.VMEM),
            pl.BlockSpec(memory_space=pltpu.VMEM),
        ],
        out_specs=pl.BlockSpec(memory_space=pltpu.VMEM),
        compiler_params=pltpu.CompilerParams(vmem_limit_bytes=32 * 1024 * 1024),
        name="pick",
    )(spots, table, weights)


def sum_kernel(terms, out, first, second, own, send1, recv1, send2, recv2, send3, recv3):
    wide, narrow = lax.axis_index("wide"), lax.axis_index("narrow")
    barrier = pltpu.get_barrier_semaphore()
    across = [(wide + d) % WIDE for d in range(1, WIDE)]
    along = [(narrow + d) % NARROW for d in range(1, NARROW)]
    for peer in across:
        pl.semaphore_signal(barrier, inc=1, device_id=(peer, narrow), device_id_type=MESH)
    for peer in along:
        pl.semaphore_signal(barrier, inc=1, device_id=(wide, peer), device_id_type=MESH)
    pl.semaphore_wait(barrier, WIDE + NARROW - 2)

    def remote(src, dst, send, recv, target):
        return pltpu.make_async_remote_copy(
            src_ref=src, dst_ref=dst, send_sem=send, recv_sem=recv, device_id=target, device_id_type=MESH
        )

    ones = [
        remote(terms.at[peer], first.at[d], send1.at[d], recv1.at[d], (peer, narrow))
        for d, peer in enumerate(across)
    ]
    for copy in ones:
        copy.start()
    value = terms[wide]
    for d, copy in enumerate(ones):
        copy.wait_recv()
        value = value + first[d]
    second[narrow] = value
    twos = [
        remote(second.at[narrow], second.at[narrow], send2.at[d], recv2.at[d], (wide, peer))
        for d, peer in enumerate(along)
    ]
    for copy in twos:
        copy.start()
    for d, copy in enumerate(twos):
        source = second.at[(narrow + NARROW - 1 - d) % NARROW]
        remote(source, source, send2.at[d], recv2.at[d], (wide, along[d])).wait_recv()
    for example in range(2):
        at = example * 4
        own[example] = (second[at] + second[at + 1]) + (second[at + 2] + second[at + 3])
    out[wide] = own[...]
    threes = [
        remote(own, out.at[wide], send3.at[d], recv3.at[d], (peer, narrow)) for d, peer in enumerate(across)
    ]
    for copy in threes:
        copy.start()
    for d, copy in enumerate(threes):
        source = out.at[(wide + WIDE - 1 - d) % WIDE]
        remote(own, source, send3.at[d], recv3.at[d], (across[d], narrow)).wait_recv()
    for copy in ones + twos + threes:
        copy.wait_send()


def sum_all(terms):
    dma = pltpu.SemaphoreType.DMA
    piece = terms.shape[1:]
    return pl.pallas_call(
        sum_kernel,
        out_shape=jax.ShapeDtypeStruct((WIDE, 2) + piece, jnp.float32),
        in_specs=[pl.BlockSpec(memory_space=pltpu.VMEM)],
        out_specs=pl.BlockSpec(memory_space=pltpu.VMEM),
        scratch_shapes=[
            pltpu.VMEM((WIDE - 1,) + piece, jnp.float32),
            pltpu.VMEM((NARROW,) + piece, jnp.float32),
            pltpu.VMEM((2,) + piece, jnp.float32),
            dma((WIDE - 1,)), dma((WIDE - 1,)), dma((NARROW - 1,)), dma((NARROW - 1,)),
            dma((WIDE - 1,)), dma((WIDE - 1,)),
        ],
        compiler_params=pltpu.CompilerParams(collective_id=1, has_side_effects=True),
        name="sum_all",
    )(terms)


def shards(hidden, out_grad, sign_bits, pick_rows, pick_cols):
    units, features = sign_bits.shape
    wide, narrow = lax.axis_index("wide"), lax.axis_index("narrow")
    signs = (2 * sign_bits - 1).astype(jnp.bfloat16)
    group, row = pick_rows // units, pick_rows % units
    block, col = pick_cols // features, pick_cols % features
    table_row = bit_parity(jnp.bitwise_and(block, 6), 3) * 4 + col // LANES
    spots = table_row * units + row
    sign = bit_parity(jnp.bitwise_and(group, wide), 4) + bit_parity(jnp.bitwise_and(block, narrow), 3)
    code = (col % LANES + LANES * jnp.bitwise_and(sign, 1)).reshape(8, 8, LANES).transpose(0, 2, 1).reshape(-1, 1)
    lanes = lax.broadcasted_iota(jnp.int32, (1, LANES), 1) + LANES
    scale = 1.0 / math.sqrt(float(SEQ) * SEQ * features * NARROW)
    weights = (1 - 2 * bit_parity(jnp.bitwise_and(code, lanes), 8)).astype(jnp.float32) * scale
    table = transform(hidden, out_grad, signs)
    terms = pick(spots, table.reshape(-1, LANES), weights)
    sums = sum_all(terms)
    return sums.reshape(WIDE, 2, -1).transpose(1, 0, 2).reshape(2, -1)


def solution(mesh):
    placed = (P("narrow", "wide"), P("wide", "narrow"), P("wide", "narrow"), P(), P())
    return jax.shard_map(shards, mesh=mesh, in_specs=placed, out_specs=P(), check_vma=False)
```

```python
import math

import jax
import jax.numpy as jnp
from jax import lax
from jax.experimental import pallas as pl
from jax.experimental.pallas import tpu as pltpu
from jax.sharding import PartitionSpec as P

SEQ = 2048
BAND = 128
LANES = 128
PIECES = 8
SPREAD = 16
BY_Z = (0,)
MESH = pl.DeviceIdType.MESH


def bit_parity(value, count):
    total = jnp.zeros_like(value)
    for bit_num in range(count):
        total = total + jnp.bitwise_and(jnp.right_shift(value, bit_num), 1)
    return jnp.bitwise_and(total, 1)


def place():
    wide, narrow = lax.axis_index("wide"), lax.axis_index("narrow")
    return wide // 8, (wide // 2) % 4, wide % 2, narrow // 2, narrow % 2


def device(z_hi, x, core, y, z_lo):
    return (z_hi * 8 + x * 2 + core, y * 2 + z_lo)


def sketch_kernel(
    acts, grads, sign_bits, pick_rows, pick_cols, out,
    hbuf, gbuf, sraw, sbuf, total, table, spots, codes, weights, spots_smem, terms, first, second, own,
    local_sem, spot_sem, hy_send, hz_send, h_recv, init_send, x_send, relay_send, g_recv,
    core_send, core_recv, s_send, s_recv, send1, recv1, send2, recv2, send3, recv3,
):
    wide, narrow = lax.axis_index("wide"), lax.axis_index("narrow")
    z_hi, x, core, y, z_lo = place()
    units = sraw.shape[0]
    y_pair = y + 1 - 2 * (y % 2)
    at_y = device(z_hi, x, core, y_pair, z_lo)
    at_z = device(z_hi, x, core, y, 1 - z_lo)
    at_far = device(z_hi, x, core, 3 - y, z_lo)
    at_hi = device(1 - z_hi, x, core, y, z_lo)
    at_hi_far = device(1 - z_hi, x, core, 3 - y, z_lo)
    at_right = device(z_hi, (x + 1) % 4, core, y, z_lo)
    at_left = device(z_hi, (x + 3) % 4, core, y, z_lo)
    at_core = device(z_hi, x, 1 - core, y, z_lo)
    holder = y // 2 == z_hi
    chunk = acts.shape[0] // 4

    piece = x * 2 + core
    member = (z_hi * 4 + y) * 2 + z_lo
    pieces = [(piece + d) % PIECES for d in range(1, PIECES)]
    members = [(member + d) % SPREAD for d in range(1, SPREAD)]
    across = [device(z_hi, t // 2, t % 2, y, z_lo) for t in pieces]
    along = [device(g // 8, x, core, (g // 2) % 4, g % 2) for g in members]

    barrier = pltpu.get_barrier_semaphore()
    for peer in across + along:
        pl.semaphore_signal(barrier, inc=1, device_id=peer, device_id_type=MESH)
    bits_in = pltpu.make_async_copy(sign_bits, sraw, local_sem.at[1])
    bits_in.start()
    own_h = pltpu.make_async_copy(acts, hbuf.at[0], local_sem.at[0])
    own_h.start()
    pl.semaphore_wait(barrier, len(across + along))

    def remote(src, dst, send, recv, target):
        return pltpu.make_async_remote_copy(
            src_ref=src, dst_ref=dst, send_sem=send, recv_sem=recv, device_id=target, device_id_type=MESH
        )

    def arrived(ref, recv):
        remote(ref, ref, s_send, recv, at_core).wait_recv()

    own_g = pltpu.make_async_copy(grads, gbuf.at[0, core, 0], local_sem.at[2])
    to_hi = remote(grads, gbuf.at[0, core, 0], init_send.at[0], g_recv.at[0, 0], at_hi)
    to_far = remote(grads, gbuf.at[0, core, 1], init_send.at[0], g_recv.at[0, 1], at_far)
    to_hi_far = remote(grads, gbuf.at[0, core, 1], init_send.at[1], g_recv.at[0, 1], at_hi_far)

    @pl.when(holder)
    def _():
        own_g.start()
        to_hi.start()

    @pl.when(jnp.logical_not(holder))
    def _():
        to_far.start()
        to_hi_far.start()

    pending = []
    by_y = tuple(num for num in range(4) if num not in BY_Z)
    for first_num, second_num in zip(BY_Z + by_y, by_y + BY_Z):
        for num, slot, sends, target in ((first_num, 1, hy_send, at_y), (second_num, 2, hz_send, at_z)):
            copy = remote(
                acts.at[pl.ds(num * chunk, chunk)], hbuf.at[slot, pl.ds(num * chunk, chunk)],
                sends.at[num], h_recv.at[slot - 1, num], target,
            )
            copy.start()
            pending.append(copy)

    def rows(slot, num):
        return hbuf.at[slot, pl.ds(num * chunk, chunk)]

    def pass_on(slot, num):
        arrived(rows(slot, num), h_recv.at[slot - 1, num])
        sends, target = ((hz_send, at_z), (hy_send, at_y))[slot - 1]
        copy = remote(rows(slot, num), rows(3, num), sends.at[4 + num], h_recv.at[2, num], target)
        copy.start()
        pending.append(copy)

    def to_sibling(slot, part):
        block = gbuf.at[slot, core, part]
        copy = remote(block, block, core_send.at[slot, part], core_recv.at[slot, part], at_core)
        copy.start()
        pending.append(copy)

    def spread(part):
        block = gbuf.at[0, core, part]
        for side, target in ((1, at_right), (2, at_left)):
            copy = remote(
                block, gbuf.at[side, core, part], x_send.at[side - 1, part], g_recv.at[side, part], target
            )
            copy.start()
            pending.append(copy)
        to_sibling(0, part)

    def around(part):
        for side in (1, 2):
            arrived(gbuf.at[side, core, part], g_recv.at[side, part])
        for side, target in ((1, at_right), (2, at_left)):

            @pl.when(core == side - 1)
            def _():
                remote(
                    gbuf.at[side, core, part], gbuf.at[3, core, part],
                    relay_send.at[part], g_recv.at[3, part], target,
                ).start()

        to_sibling(1, part)
        to_sibling(2, part)

    bits_in.wait()

    def to_sign(group, carry):
        band = pl.ds(pl.multiple_of(group * BAND, BAND), BAND)
        sbuf[0, band, :] = (2 * sraw[band, :] - 1).astype(jnp.float32).astype(jnp.bfloat16)
        return carry

    lax.fori_loop(0, units // BAND, to_sign, 0)

    sampled, features = pick_rows[...], pick_cols[...]
    group = jnp.zeros_like(sampled)
    for num in range(1, 16):
        group = group + (sampled >= num * units).astype(jnp.int32)
    block, col = features // 512, features % 512
    upper = bit_parity(jnp.bitwise_and(block, 6), 3)
    spot = (upper * 4 + col // LANES) * units + sampled - group * units
    ahead_of = (lax.broadcasted_iota(jnp.int32, (8, LANES), 1) // 16 + 8 - lax.broadcasted_iota(jnp.int32, (8, LANES), 0)) % 8
    for tile in range(PIECES):
        straight = spot[tile * 8:(tile + 1) * 8]
        turned = straight
        for d in range(1, 8):
            turned = jnp.where(ahead_of == d, pltpu.roll(pltpu.roll(straight, 8 - d, 0), 16 * d, 1), turned)
        for part in range(4):
            spots[tile * 4 + part] = turned[2 * part:2 * part + 2]
    sign = bit_parity(jnp.bitwise_and(group, wide), 4) + bit_parity(jnp.bitwise_and(block, narrow), 3)
    codes[...] = col % LANES + LANES * (sign % 2)

    lane_bits = lax.broadcasted_iota(jnp.int32, (8, LANES), 1) + LANES

    def weigh(first_tile, last_tile):
        def some(num, code):
            for inner in range(16):
                odd = jnp.bitwise_and(jnp.broadcast_to(code[:, inner:inner + 1], (8, LANES)), lane_bits)
                odd = jnp.bitwise_and(lax.population_count(odd), 1)
                weights[num // 8, num % 8 * 16 + inner] = jnp.where(odd == 1, -1.0, 1.0).astype(jnp.float32)
            code = pltpu.roll(code, LANES - 16, 1)
            after = jnp.minimum(num // 8 + 1, PIECES - 1)
            return jnp.where(num % 8 == 7, codes[pl.ds(pl.multiple_of(after * 8, 8), 8), :], code)

        lax.fori_loop(first_tile * 8, last_tile * 8, some, codes[first_tile * 8:(first_tile + 1) * 8, :])

    def spots_part(d, part):
        tile = lax.rem(piece + 1 + d, PIECES)
        return pltpu.make_async_copy(spots.at[tile * 4 + part], spots_smem.at[part], spot_sem.at[part])

    @pl.when(holder)
    def _():
        own_g.wait()

    @pl.when(jnp.logical_not(holder))
    def _():
        arrived(gbuf.at[0, core, 0], g_recv.at[0, 0])

    spread(0)
    send_s = remote(sbuf.at[0], sbuf.at[1], s_send, s_recv, at_far)
    send_s.start()
    weigh(0, 2)
    pass_on(1, BY_Z[0])
    pass_on(2, by_y[0])
    weigh(2, 4)
    arrived(gbuf.at[0, core, 1], g_recv.at[0, 1])
    spread(1)
    for num in BY_Z[1:]:
        pass_on(1, num)
    pass_on(2, by_y[1])
    weigh(4, 6)
    around(0)
    weigh(6, 8)
    for num in by_y[2:]:
        pass_on(2, num)
    around(1)
    for part in range(2):
        arrived(gbuf.at[3, core, part], g_recv.at[3, part])
        to_sibling(3, part)

    total[...] = jnp.zeros_like(total)
    own_h.wait()
    for slot in range(4):
        for part in range(2):
            arrived(gbuf.at[slot, 1 - core, part], core_recv.at[slot, part])

    y_bit, depth = y % 2, acts.shape[0] // 2

    def step(num, carry):
        slot, half = num // 2, num % 2
        for which in (1, 2, 3):
            for one in range(4):
                if not ((which == 1 and one in BY_Z) or (which == 2 and one in by_y)):

                    @pl.when(num == 2 * which + one // 2)
                    def _():
                        arrived(rows(which, one), h_recv.at[which - 1, one])

        from_y, from_z = slot % 2, slot // 2
        tokens = ((y_bit + from_y) % 2) * 2 + (z_lo + from_z) % 2
        ahead = (tokens - x + 4) % 4
        source = (ahead + (ahead + 1) // 2) % 4
        left = hbuf[slot, pl.ds(pl.multiple_of(half * depth, depth), depth), :]
        for part in range(2):
            total[part] += lax.dot_general(
                left, gbuf[source, half, part], (((0,), (0,)), ((), ())), preferred_element_type=jnp.float32
            )
        return carry

    for part in range(4):
        spots_part(0, part).start()
    lax.fori_loop(0, 8, step, 0)
    arrived(sbuf.at[1], s_recv)

    row_nums = lax.broadcasted_iota(jnp.int32, (BAND, 2 * BAND), 0)
    col_nums = lax.broadcasted_iota(jnp.int32, (BAND, 2 * BAND), 1)
    walsh = (1 - 2 * bit_parity(jnp.bitwise_and(row_nums, col_nums), 7)).astype(jnp.float32).astype(jnp.bfloat16)

    def mix(group, carry):
        band = pl.ds(pl.multiple_of(group * BAND, BAND), BAND)
        values = []
        for part in range(2):
            flipped = total[part, band, :] * sbuf[part, band, :].astype(jnp.float32)
            high = flipped.astype(jnp.bfloat16)
            low = (flipped - high.astype(jnp.float32)).astype(jnp.bfloat16)
            both = jnp.concatenate([high, low], axis=0)
            mixed = jnp.dot(walsh, both, preferred_element_type=jnp.float32)
            values += [mixed[:, k * LANES:(k + 1) * LANES] for k in range(4)]
        for stride in (1, 2, 4):
            values = [
                values[k - stride] - values[k] if k & stride else values[k] + values[k + stride]
                for k in range(8)
            ]
        for k in range(8):
            table[pl.ds(pl.multiple_of(k * units + group * BAND, BAND), BAND), :] = values[k]
        return carry

    lax.fori_loop(0, units // BAND, mix, 0)

    lane_nums = lax.broadcasted_iota(jnp.int32, (8, LANES), 1)
    sub_nums = lax.broadcasted_iota(jnp.int32, (8, LANES), 0)

    def pick(d, carry):
        tile = lax.rem(piece + 1 + d, PIECES)
        found = jnp.zeros((8, LANES), jnp.float32)
        for part in range(4):
            spots_part(d, part).wait()
            for num in (2 * part, 2 * part + 1):
                for inner in range(16):
                    for sub in range(8):
                        spot = spots_smem[part, num % 2, sub * 16 + inner]
                        row = jnp.broadcast_to(table[pl.ds(spot, 1), :], (8, LANES))
                        taken = row if sub == 0 else jnp.where(sub_nums == sub, row, taken)
                    lane = num * 16 + inner
                    value = jnp.sum(taken * weights[tile, lane], axis=1, keepdims=True)
                    found = jnp.where(lane_nums == lane, value, found)

            @pl.when(d < PIECES - 1)
            def _():
                spots_part(d + 1, part).start()

        for num in range(1, PIECES):

            @pl.when(d == num)
            def _():
                ones[num - 1].start()

        terms[d] = found
        return carry

    ones = [
        remote(terms.at[d], first.at[d], send1.at[d], recv1.at[d], across[d]) for d in range(PIECES - 1)
    ]
    lax.fori_loop(0, PIECES, pick, 0)
    value = terms[PIECES - 1]
    for d, copy in enumerate(ones):
        copy.wait_recv()
        value = value + first[d]
    second[member] = value
    twos = [
        remote(second.at[member], second.at[member], send2.at[d], recv2.at[d], along[d]) for d in range(SPREAD - 1)
    ]
    for copy in twos:
        copy.start()
    for d in range(SPREAD - 1):
        source = second.at[(member + SPREAD - 1 - d) % SPREAD]
        remote(source, source, send2.at[d], recv2.at[d], along[d]).wait_recv()
    scale = 1.0 / math.sqrt(float(SEQ) * SEQ * 4096)
    for example in range(2):
        parts = [second[8 * hi + 4 * example + num] for hi in range(2) for num in range(4)]
        while len(parts) > 1:
            parts = [parts[k] + parts[k + 1] for k in range(0, len(parts), 2)]
        own[example] = parts[0] * scale
    out[piece] = own[...]
    threes = [
        remote(own, out.at[piece], send3.at[d], recv3.at[d], across[d]) for d in range(PIECES - 1)
    ]
    for copy in threes:
        copy.start()
    for d in range(PIECES - 1):
        source = out.at[(piece + PIECES - 1 - d) % PIECES]
        remote(own, source, send3.at[d], recv3.at[d], across[d]).wait_recv()

    for copy in pending + ones + twos + threes:
        copy.wait_send()
    send_s.wait_send()
    for part in range(2):
        remote(
            gbuf.at[1, core, part], gbuf.at[3, core, part], relay_send.at[part], g_recv.at[3, part], at_core
        ).wait_send()
    to_hi.wait_send()

    @pl.when(jnp.logical_not(holder))
    def _():
        to_hi_far.wait_send()


def shards(hidden, out_grad, sign_bits, pick_rows, pick_cols):
    units, features = sign_bits.shape
    tokens = hidden.shape[0]
    part_tokens = out_grad.shape[0]
    dma = pltpu.SemaphoreType.DMA
    tile = (8, LANES)
    hbm, vmem = pl.BlockSpec(memory_space=pltpu.HBM), pl.BlockSpec(memory_space=pltpu.VMEM)
    sums = pl.pallas_call(
        sketch_kernel,
        out_shape=jax.ShapeDtypeStruct((PIECES, 2) + tile, jnp.float32),
        in_specs=[hbm, hbm, hbm, vmem, vmem],
        out_specs=vmem,
        scratch_shapes=[
            pltpu.VMEM((4, tokens, units), jnp.bfloat16),
            pltpu.VMEM((4, 2, 2, part_tokens, features), jnp.bfloat16),
            pltpu.VMEM((units, features), jnp.int32),
            pltpu.VMEM((2, units, features), jnp.bfloat16),
            pltpu.VMEM((2, units, features), jnp.float32),
            pltpu.VMEM((8 * units, LANES), jnp.float32),
            pltpu.VMEM((PIECES * 4, 2, LANES), jnp.int32),
            pltpu.VMEM((PIECES * 8, LANES), jnp.int32),
            pltpu.VMEM((PIECES, LANES) + tile, jnp.float32),
            pltpu.SMEM((4, 2, LANES), jnp.int32),
            pltpu.VMEM((PIECES,) + tile, jnp.float32),
            pltpu.VMEM((PIECES - 1,) + tile, jnp.float32),
            pltpu.VMEM((SPREAD,) + tile, jnp.float32),
            pltpu.VMEM((2,) + tile, jnp.float32),
            dma((3,)), dma((4,)), dma((8,)), dma((8,)), dma((3, 4)), dma((2,)), dma((2, 2)), dma((2,)), dma((4, 2)),
            dma((4, 2)), dma((4, 2)), dma, dma,
            dma((PIECES - 1,)), dma((PIECES - 1,)), dma((SPREAD - 1,)), dma((SPREAD - 1,)),
            dma((PIECES - 1,)), dma((PIECES - 1,)),
        ],
        compiler_params=pltpu.CompilerParams(
            collective_id=0, has_side_effects=True, vmem_limit_bytes=62 * 1024 * 1024
        ),
        name="sketch",
    )(hidden, out_grad, sign_bits, pick_rows.reshape(-1, LANES), pick_cols.reshape(-1, LANES))
    return sums.transpose(1, 0, 2, 3).reshape(2, -1)


def solution(mesh):
    placed = (P("narrow", "wide"), P("wide", "narrow"), P("wide", "narrow"), P(), P())
    return jax.shard_map(shards, mesh=mesh, in_specs=placed, out_specs=P(), check_vma=False)
```

```python
import math

import jax
import jax.numpy as jnp
from jax import lax
from jax.experimental import pallas as pl
from jax.experimental.pallas import tpu as pltpu
from jax.sharding import PartitionSpec as P

SEQ = 2048
BAND = 128
LANES = 128
PIECES = 8
SPREAD = 16
CHUNKS = 8
BY_Z = (0, 1)
MESH = pl.DeviceIdType.MESH


def bit_parity(value, count):
    total = jnp.zeros_like(value)
    for bit_num in range(count):
        total = total + jnp.bitwise_and(jnp.right_shift(value, bit_num), 1)
    return jnp.bitwise_and(total, 1)


def div(value, by):
    return lax.div(value, jnp.int32(by))


def mod(value, by):
    return lax.rem(value, jnp.int32(by))


def place():
    wide, narrow = lax.axis_index("wide"), lax.axis_index("narrow")
    return div(wide, 8), mod(div(wide, 2), 4), mod(wide, 2), div(narrow, 2), mod(narrow, 2)


def device(z_hi, x, core, y, z_lo):
    return (z_hi * 8 + x * 2 + core, y * 2 + z_lo)


def sketch_kernel(
    acts, grads, sign_bits, pick_rows, pick_cols, out,
    picks, hbuf, gbuf, sraw, sbuf, total, table, spots, codes, weights, spots_smem, terms, first, second, own,
    local_sem, spot_sem, hy_send, hz_send, h_recv, init_send, x_send, relay_send, g_recv,
    core_send, core_recv, s_send, s_recv, send1, recv1, send2, recv2, send3, recv3,
):
    wide, narrow = lax.axis_index("wide"), lax.axis_index("narrow")
    z_hi, x, core, y, z_lo = place()
    units = sraw.shape[0]
    y_bit, upper_y = mod(y, 2), div(y, 2)
    y_pair = y + 1 - 2 * y_bit
    at_y = device(z_hi, x, core, y_pair, z_lo)
    at_z = device(z_hi, x, core, y, 1 - z_lo)
    at_far = device(z_hi, x, core, 3 - y, z_lo)
    at_hi = device(1 - z_hi, x, core, y, z_lo)
    at_hi_far = device(1 - z_hi, x, core, 3 - y, z_lo)
    at_right = device(z_hi, mod(x + 1, 4), core, y, z_lo)
    at_left = device(z_hi, mod(x + 3, 4), core, y, z_lo)
    at_core = device(z_hi, x, 1 - core, y, z_lo)
    holder = upper_y == z_hi
    chunk = acts.shape[0] // CHUNKS

    piece = x * 2 + core
    member = (z_hi * 4 + y) * 2 + z_lo
    pieces = [mod(piece + d, PIECES) for d in range(1, PIECES)]
    members = [mod(member + d, SPREAD) for d in range(1, SPREAD)]
    across = [(z_hi * 8 + t, narrow) for t in pieces]
    along = [(div(g, 8) * 8 + piece, mod(g, 8)) for g in members]

    barrier = pltpu.get_barrier_semaphore()
    for peer in across + along:
        pl.semaphore_signal(barrier, inc=1, device_id=peer, device_id_type=MESH)
    bits_in = pltpu.make_async_copy(sign_bits, sraw, local_sem.at[1])
    bits_in.start()
    own_h = pltpu.make_async_copy(acts, hbuf.at[0], local_sem.at[0])
    own_h.start()
    picks_in = [
        pltpu.make_async_copy(source, picks.at[num], local_sem.at[3 + num])
        for num, source in enumerate((pick_rows, pick_cols))
    ]
    for copy in picks_in:
        copy.start()
    pl.semaphore_wait(barrier, len(across + along))

    def remote(src, dst, send, recv, target):
        return pltpu.make_async_remote_copy(
            src_ref=src, dst_ref=dst, send_sem=send, recv_sem=recv, device_id=target, device_id_type=MESH
        )

    def arrived(ref, recv):
        remote(ref, ref, s_send, recv, at_core).wait_recv()

    own_g = pltpu.make_async_copy(grads, gbuf.at[0, core, 0], local_sem.at[2])
    to_hi = remote(grads, gbuf.at[0, core, 0], init_send.at[0], g_recv.at[0, 0], at_hi)
    to_far = remote(grads, gbuf.at[0, core, 1], init_send.at[0], g_recv.at[0, 1], at_far)
    to_hi_far = remote(grads, gbuf.at[0, core, 1], init_send.at[1], g_recv.at[0, 1], at_hi_far)

    @pl.when(holder)
    def _():
        own_g.start()
        to_hi.start()

    @pl.when(jnp.logical_not(holder))
    def _():
        to_far.start()
        to_hi_far.start()

    pending = []
    by_y = tuple(num for num in range(CHUNKS) if num not in BY_Z)
    for first_num, second_num in zip(BY_Z + by_y, by_y + BY_Z):
        for num, slot, sends, target in ((first_num, 1, hy_send, at_y), (second_num, 2, hz_send, at_z)):
            copy = remote(
                acts.at[pl.ds(num * chunk, chunk)], hbuf.at[slot, pl.ds(num * chunk, chunk)],
                sends.at[num], h_recv.at[slot - 1, num], target,
            )
            copy.start()
            pending.append(copy)

    def rows(slot, num):
        return hbuf.at[slot, pl.ds(num * chunk, chunk)]

    def pass_on(slot, num):
        arrived(rows(slot, num), h_recv.at[slot - 1, num])
        sends, target = ((hz_send, at_z), (hy_send, at_y))[slot - 1]
        copy = remote(rows(slot, num), rows(3, num), sends.at[CHUNKS + num], h_recv.at[2, num], target)
        copy.start()
        pending.append(copy)

    def to_sibling(slot, part):
        block = gbuf.at[slot, core, part]
        copy = remote(block, block, core_send.at[slot, part], core_recv.at[slot, part], at_core)
        copy.start()
        pending.append(copy)

    def spread(part):
        block = gbuf.at[0, core, part]
        for side, target in ((1, at_right), (2, at_left)):
            copy = remote(
                block, gbuf.at[side, core, part], x_send.at[side - 1, part], g_recv.at[side, part], target
            )
            copy.start()
            pending.append(copy)
        to_sibling(0, part)

    def around(part):
        for side in (1, 2):
            arrived(gbuf.at[side, core, part], g_recv.at[side, part])
        for side, target in ((1, at_right), (2, at_left)):

            @pl.when(core == side - 1)
            def _():
                remote(
                    gbuf.at[side, core, part], gbuf.at[3, core, part],
                    relay_send.at[part], g_recv.at[3, part], target,
                ).start()

        to_sibling(1, part)
        to_sibling(2, part)

    bits_in.wait()

    def to_sign(group, carry):
        band = pl.ds(pl.multiple_of(group * BAND, BAND), BAND)
        sbuf[0, band, :] = (2 * sraw[band, :] - 1).astype(jnp.float32).astype(jnp.bfloat16)
        return carry

    lax.fori_loop(0, units // BAND, to_sign, 0)

    send_s = remote(sbuf.at[0], sbuf.at[1], s_send, s_recv, at_far)
    for copy in picks_in:
        copy.wait()
    sampled, features = picks[0], picks[1]
    group = jnp.zeros_like(sampled)
    for num in range(1, 16):
        group = group + (sampled >= num * units).astype(jnp.int32)
    block, col = features // 512, features % 512
    upper = bit_parity(jnp.bitwise_and(block, 6), 3)
    spot = (upper * 4 + col // LANES) * units + sampled - group * units
    ahead_of = (lax.broadcasted_iota(jnp.int32, (8, LANES), 1) // 16 + 8 - lax.broadcasted_iota(jnp.int32, (8, LANES), 0)) % 8
    for tile in range(PIECES):
        straight = spot[tile * 8:(tile + 1) * 8]
        turned = straight
        for d in range(1, 8):
            turned = jnp.where(ahead_of == d, pltpu.roll(pltpu.roll(straight, 8 - d, 0), 16 * d, 1), turned)
        for part in range(4):
            spots[tile * 4 + part] = turned[2 * part:2 * part + 2]
    sign = bit_parity(jnp.bitwise_and(group, wide), 4) + bit_parity(jnp.bitwise_and(block, narrow), 3)
    codes[...] = col % LANES + LANES * (sign % 2)

    lane_bits = lax.broadcasted_iota(jnp.int32, (8, LANES), 1) + LANES

    def weigh(first_tile, last_tile):
        def some(num, code):
            for inner in range(16):
                odd = jnp.bitwise_and(jnp.broadcast_to(code[:, inner:inner + 1], (8, LANES)), lane_bits)
                odd = jnp.bitwise_and(lax.population_count(odd), 1)
                weights[num // 8, num % 8 * 16 + inner] = jnp.where(odd == 1, -1.0, 1.0).astype(jnp.float32)
            code = pltpu.roll(code, LANES - 16, 1)
            after = jnp.minimum(num // 8 + 1, PIECES - 1)
            return jnp.where(num % 8 == 7, codes[pl.ds(pl.multiple_of(after * 8, 8), 8), :], code)

        lax.fori_loop(first_tile * 8, last_tile * 8, some, codes[first_tile * 8:(first_tile + 1) * 8, :])

    def spots_part(d, part):
        tile = lax.rem(piece + 1 + d, PIECES)
        return pltpu.make_async_copy(spots.at[tile * 4 + part], spots_smem.at[part], spot_sem.at[part])

    send_s.start()

    @pl.when(holder)
    def _():
        own_g.wait()

    @pl.when(jnp.logical_not(holder))
    def _():
        arrived(gbuf.at[0, core, 0], g_recv.at[0, 0])

    def half_of(nums, which):
        middle = (len(nums) + 1) // 2
        return nums[:middle] if which == 0 else nums[middle:]

    spread(0)
    weigh(0, 3)
    arrived(gbuf.at[0, core, 1], g_recv.at[0, 1])
    spread(1)
    weigh(3, 6)
    for num in half_of(BY_Z, 0):
        pass_on(1, num)
    around(0)
    weigh(6, 8)
    early, late = half_of(by_y, 0), half_of(by_y, 1)
    for num in half_of(early, 0):
        pass_on(2, num)
    for num in half_of(BY_Z, 1):
        pass_on(1, num)
    around(1)
    for num in half_of(early, 1):
        pass_on(2, num)
    arrived(gbuf.at[3, core, 0], g_recv.at[3, 0])
    to_sibling(3, 0)
    for num in half_of(late, 0):
        pass_on(2, num)
    arrived(gbuf.at[3, core, 1], g_recv.at[3, 1])
    to_sibling(3, 1)
    for num in half_of(late, 1):
        pass_on(2, num)

    total[...] = jnp.zeros_like(total)
    own_h.wait()
    for slot in range(4):
        for part in range(2):
            arrived(gbuf.at[slot, 1 - core, part], core_recv.at[slot, part])

    depth = acts.shape[0] // 2

    def step(num, carry):
        slot, half = div(num, 2), mod(num, 2)
        for which in (1, 2, 3):
            for one in range(CHUNKS):
                if not ((which == 1 and one in BY_Z) or (which == 2 and one in by_y)):

                    @pl.when(num == 2 * which + one // (CHUNKS // 2))
                    def _():
                        arrived(rows(which, one), h_recv.at[which - 1, one])

        from_y, from_z = mod(slot, 2), div(slot, 2)
        tokens = mod(y_bit + from_y, 2) * 2 + mod(z_lo + from_z, 2)
        ahead = mod(tokens - x + 4, 4)
        source = mod(ahead + div(ahead + 1, 2), 4)
        left = hbuf[slot, pl.ds(pl.multiple_of(half * depth, depth), depth), :]
        for part in range(2):
            total[part] += lax.dot_general(
                left, gbuf[source, half, part], (((0,), (0,)), ((), ())), preferred_element_type=jnp.float32
            )
        return carry

    for part in range(4):
        spots_part(0, part).start()
    lax.fori_loop(0, 8, step, 0)
    arrived(sbuf.at[1], s_recv)

    row_nums = lax.broadcasted_iota(jnp.int32, (BAND, 2 * BAND), 0)
    col_nums = lax.broadcasted_iota(jnp.int32, (BAND, 2 * BAND), 1)
    walsh = (1 - 2 * bit_parity(jnp.bitwise_and(row_nums, col_nums), 7)).astype(jnp.float32).astype(jnp.bfloat16)

    def mix(group, carry):
        band = pl.ds(pl.multiple_of(group * BAND, BAND), BAND)
        values = []
        for part in range(2):
            flipped = total[part, band, :] * sbuf[part, band, :].astype(jnp.float32)
            high = flipped.astype(jnp.bfloat16)
            low = (flipped - high.astype(jnp.float32)).astype(jnp.bfloat16)
            both = jnp.concatenate([high, low], axis=0)
            mixed = jnp.dot(walsh, both, preferred_element_type=jnp.float32)
            values += [mixed[:, k * LANES:(k + 1) * LANES] for k in range(4)]
        for stride in (1, 2, 4):
            values = [
                values[k - stride] - values[k] if k & stride else values[k] + values[k + stride]
                for k in range(8)
            ]
        for k in range(8):
            table[pl.ds(pl.multiple_of(k * units + group * BAND, BAND), BAND), :] = values[k]
        return carry

    lax.fori_loop(0, units // BAND, mix, 0)

    lane_nums = lax.broadcasted_iota(jnp.int32, (8, LANES), 1)
    sub_nums = lax.broadcasted_iota(jnp.int32, (8, LANES), 0)

    def pick(d, carry):
        tile = lax.rem(piece + 1 + d, PIECES)
        found = jnp.zeros((8, LANES), jnp.float32)
        for part in range(4):
            spots_part(d, part).wait()
            for num in (2 * part, 2 * part + 1):
                for inner in range(16):
                    for sub in range(8):
                        spot = spots_smem[part, num % 2, sub * 16 + inner]
                        row = jnp.broadcast_to(table[pl.ds(spot, 1), :], (8, LANES))
                        taken = row if sub == 0 else jnp.where(sub_nums == sub, row, taken)
                    lane = num * 16 + inner
                    value = jnp.sum(taken * weights[tile, lane], axis=1, keepdims=True)
                    found = jnp.where(lane_nums == lane, value, found)

            @pl.when(d < PIECES - 1)
            def _():
                spots_part(d + 1, part).start()

            if part == 0:
                for num in range(1, PIECES):

                    @pl.when(d == num)
                    def _():
                        ones[num - 1].start()

        terms[d] = found
        return carry

    ones = [
        remote(terms.at[d], first.at[d], send1.at[d], recv1.at[d], across[d]) for d in range(PIECES - 1)
    ]
    lax.fori_loop(0, PIECES, pick, 0)
    value = terms[PIECES - 1]
    for d, copy in enumerate(ones):
        copy.wait_recv()
        value = value + first[d]
    second[member] = value
    twos = [
        remote(second.at[member], second.at[member], send2.at[d], recv2.at[d], along[d]) for d in range(SPREAD - 1)
    ]
    for copy in twos:
        copy.start()
    for d in range(SPREAD - 1):
        source = second.at[mod(member + SPREAD - 1 - d, SPREAD)]
        remote(source, source, send2.at[d], recv2.at[d], along[d]).wait_recv()
    scale = 1.0 / math.sqrt(float(SEQ) * SEQ * 4096)
    for example in range(2):
        parts = [second[8 * hi + 4 * example + num] for hi in range(2) for num in range(4)]
        while len(parts) > 1:
            parts = [parts[k] + parts[k + 1] for k in range(0, len(parts), 2)]
        own[example] = parts[0] * scale
    for example in range(2):
        out[example, piece] = own[example]
    threes = [
        remote(own, out.at[:, piece], send3.at[d], recv3.at[d], across[d]) for d in range(PIECES - 1)
    ]
    for copy in threes:
        copy.start()
    for d in range(PIECES - 1):
        source = out.at[:, mod(piece + PIECES - 1 - d, PIECES)]
        remote(own, source, send3.at[d], recv3.at[d], across[d]).wait_recv()

    for copy in pending + ones + twos + threes:
        copy.wait_send()
    send_s.wait_send()
    for part in range(2):
        remote(
            gbuf.at[1, core, part], gbuf.at[3, core, part], relay_send.at[part], g_recv.at[3, part], at_core
        ).wait_send()
    to_hi.wait_send()

    @pl.when(jnp.logical_not(holder))
    def _():
        to_hi_far.wait_send()


def shards(hidden, out_grad, sign_bits, pick_rows, pick_cols):
    units, features = sign_bits.shape
    tokens = hidden.shape[0]
    part_tokens = out_grad.shape[0]
    dma = pltpu.SemaphoreType.DMA
    tile = (8, LANES)
    hbm, vmem = pl.BlockSpec(memory_space=pltpu.HBM), pl.BlockSpec(memory_space=pltpu.VMEM)
    sums = pl.pallas_call(
        sketch_kernel,
        out_shape=jax.ShapeDtypeStruct((2, PIECES) + tile, jnp.float32),
        in_specs=[hbm] * 5,
        out_specs=vmem,
        scratch_shapes=[
            pltpu.VMEM((2, PIECES * 8, LANES), jnp.int32),
            pltpu.VMEM((4, tokens, units), jnp.bfloat16),
            pltpu.VMEM((4, 2, 2, part_tokens, features), jnp.bfloat16),
            pltpu.VMEM((units, features), jnp.int32),
            pltpu.VMEM((2, units, features), jnp.bfloat16),
            pltpu.VMEM((2, units, features), jnp.float32),
            pltpu.VMEM((8 * units, LANES), jnp.float32),
            pltpu.VMEM((PIECES * 4, 2, LANES), jnp.int32),
            pltpu.VMEM((PIECES * 8, LANES), jnp.int32),
            pltpu.VMEM((PIECES, LANES) + tile, jnp.float32),
            pltpu.SMEM((4, 2, LANES), jnp.int32),
            pltpu.VMEM((PIECES,) + tile, jnp.float32),
            pltpu.VMEM((PIECES - 1,) + tile, jnp.float32),
            pltpu.VMEM((SPREAD,) + tile, jnp.float32),
            pltpu.VMEM((2,) + tile, jnp.float32),
            dma((5,)), dma((4,)), dma((2 * CHUNKS,)), dma((2 * CHUNKS,)), dma((3, CHUNKS)), dma((2,)), dma((2, 2)), dma((2,)), dma((4, 2)),
            dma((4, 2)), dma((4, 2)), dma, dma,
            dma((PIECES - 1,)), dma((PIECES - 1,)), dma((SPREAD - 1,)), dma((SPREAD - 1,)),
            dma((PIECES - 1,)), dma((PIECES - 1,)),
        ],
        compiler_params=pltpu.CompilerParams(
            collective_id=0, has_side_effects=True, vmem_limit_bytes=62 * 1024 * 1024
        ),
        name="sketch",
    )(hidden, out_grad, sign_bits, pick_rows.reshape(-1, LANES), pick_cols.reshape(-1, LANES))
    return sums.reshape(2, -1)


def solution(mesh):
    placed = (P("narrow", "wide"), P("wide", "narrow"), P("wide", "narrow"), P(), P())
    return jax.shard_map(shards, mesh=mesh, in_specs=placed, out_specs=P(), check_vma=False)
```

```python
import math

import jax
import jax.numpy as jnp
from jax import lax
from jax.experimental import pallas as pl
from jax.experimental.pallas import tpu as pltpu
from jax.sharding import PartitionSpec as P

SEQ = 2048
BAND = 128
LANES = 128
PIECES = 8
SPREAD = 16
UNITS = 4
CHUNKS = 8
BY_Z = (0, 1, 2)
LEAD = 2
MESH = pl.DeviceIdType.MESH


def bit_parity(value, count):
    total = jnp.zeros_like(value)
    for bit_num in range(count):
        total = total + jnp.bitwise_and(jnp.right_shift(value, bit_num), 1)
    return jnp.bitwise_and(total, 1)


def div(value, by):
    return lax.div(value, jnp.int32(by))


def mod(value, by):
    return lax.rem(value, jnp.int32(by))


def place():
    wide, narrow = lax.axis_index("wide"), lax.axis_index("narrow")
    return div(wide, 8), mod(div(wide, 2), 4), mod(wide, 2), div(narrow, 2), mod(narrow, 2)


def device(z_hi, x, core, y, z_lo):
    return (z_hi * 8 + x * 2 + core, y * 2 + z_lo)


def sketch_kernel(
    acts, grads, sign_bits, pick_rows, pick_cols, out,
    picks, hbuf, gbuf, transit, sraw, sbuf, total, table, spots, codes, weights, spots_smem, terms, first, second, own,
    local_sem, spot_sem, hy_send, hz_send, h_recv, init_send, far_send, t_send, t_recv, x_send, relay_send, g_recv,
    core_send, core_recv, s_send, s_recv, send1, recv1, send2, recv2, send3, recv3,
):
    wide, narrow = lax.axis_index("wide"), lax.axis_index("narrow")
    z_hi, x, core, y, z_lo = place()
    units = sraw.shape[0]
    y_bit, upper_y = mod(y, 2), div(y, 2)
    y_pair = y + 1 - 2 * y_bit
    at_y = device(z_hi, x, core, y_pair, z_lo)
    at_z = device(z_hi, x, core, y, 1 - z_lo)
    at_far = device(z_hi, x, core, 3 - y, z_lo)
    at_cross = device(1 - z_hi, x, core, y, 1 - z_lo)
    at_right = device(z_hi, mod(x + 1, 4), core, y, z_lo)
    at_left = device(z_hi, mod(x + 3, 4), core, y, z_lo)
    at_core = device(z_hi, x, 1 - core, y, z_lo)
    holder = upper_y == z_hi
    chunk = acts.shape[0] // CHUNKS

    piece = x * 2 + core
    member = (z_hi * 4 + y) * 2 + z_lo
    pieces = [mod(piece + d, PIECES) for d in range(1, PIECES)]
    members = [mod(member + d, SPREAD) for d in range(1, SPREAD)]
    across = [(z_hi * 8 + t, narrow) for t in pieces]
    along = [(div(g, 8) * 8 + piece, mod(g, 8)) for g in members]

    barrier = pltpu.get_barrier_semaphore()
    for peer in across + along:
        pl.semaphore_signal(barrier, inc=1, device_id=peer, device_id_type=MESH)
    bits_in = pltpu.make_async_copy(sign_bits, sraw, local_sem.at[1])
    bits_in.start()
    own_h = pltpu.make_async_copy(acts, hbuf.at[0], local_sem.at[0])
    own_h.start()
    picks_in = [
        pltpu.make_async_copy(source, picks.at[num], local_sem.at[3 + num])
        for num, source in enumerate((pick_rows, pick_cols))
    ]
    for copy in picks_in:
        copy.start()
    pl.semaphore_wait(barrier, len(across + along))

    def remote(src, dst, send, recv, target):
        return pltpu.make_async_remote_copy(
            src_ref=src, dst_ref=dst, send_sem=send, recv_sem=recv, device_id=target, device_id_type=MESH
        )

    def arrived(ref, recv):
        remote(ref, ref, s_send, recv, at_core).wait_recv()

    own_g = pltpu.make_async_copy(grads, gbuf.at[0, core, 0], local_sem.at[2])
    few = grads.shape[0] // 2

    def piece_of(ref, unit):
        return ref.at[pl.ds(unit % 2 * few, few)]

    def unit_at(slot, half, unit):
        return gbuf.at[slot, half, unit // 2, pl.ds(unit % 2 * few, few)]

    follower = jnp.logical_not(holder)
    cross = [
        remote(piece_of(grads, unit), transit.at[unit], init_send.at[unit], t_recv.at[unit], at_cross)
        for unit in range(2)
    ]
    to_far = [
        remote(piece_of(grads, unit), unit_at(0, core, 2 + unit), far_send.at[unit], g_recv.at[0, 2 + unit], at_far)
        for unit in range(2)
    ]
    hand_on = [
        remote(transit.at[unit], unit_at(0, core, unit), t_send.at[unit], g_recv.at[0, unit], at_z)
        for unit in range(2)
    ]
    hand_over = [
        remote(transit.at[unit], transit.at[2 + unit], t_send.at[unit], t_recv.at[2 + unit], at_z)
        for unit in range(2)
    ]
    onward = [
        remote(
            transit.at[2 + unit], unit_at(0, core, 2 + unit), far_send.at[unit], g_recv.at[0, 2 + unit], at_far
        )
        for unit in range(2)
    ]
    for copy in cross:
        copy.start()

    @pl.when(holder)
    def _():
        own_g.start()

    @pl.when(follower)
    def _():
        for copy in to_far:
            copy.start()

    pending = []
    by_y = tuple(num for num in range(CHUNKS) if num not in BY_Z)
    def activations(slot, num):
        sends, target = ((hy_send, at_y), (hz_send, at_z))[slot - 1]
        copy = remote(
            acts.at[pl.ds(num * chunk, chunk)], hbuf.at[slot, pl.ds(num * chunk, chunk)],
            sends.at[num], h_recv.at[slot - 1, num], target,
        )
        pending.append(copy)
        return copy

    by_z_pair = [activations(2, num) for num in by_y + BY_Z]
    for copy in by_z_pair[:LEAD]:
        copy.start()
    for num in BY_Z + by_y:
        activations(1, num).start()

    def rows(slot, num):
        return hbuf.at[slot, pl.ds(num * chunk, chunk)]

    def pass_on(slot, num):
        arrived(rows(slot, num), h_recv.at[slot - 1, num])
        sends, target = ((hz_send, at_z), (hy_send, at_y))[slot - 1]
        copy = remote(rows(slot, num), rows(3, num), sends.at[CHUNKS + num], h_recv.at[2, num], target)
        copy.start()
        pending.append(copy)

    def to_sibling(slot, unit):
        block = unit_at(slot, core, unit)
        copy = remote(block, block, core_send.at[slot, unit], core_recv.at[slot, unit], at_core)
        pending.append(copy)
        return copy

    spreads = [
        [
            remote(
                unit_at(0, core, unit), unit_at(side, core, unit), x_send.at[side - 1, unit],
                g_recv.at[side, unit], target,
            )
            for side, target in ((1, at_right), (2, at_left))
        ]
        for unit in range(UNITS)
    ]
    for copies in spreads:
        pending.extend(copies)
    own_siblings = [to_sibling(0, unit) for unit in range(UNITS)]

    def spread(unit):
        for copy in spreads[unit]:
            copy.start()
        own_siblings[unit].start()

    def around(unit):
        for side in (1, 2):
            arrived(unit_at(side, core, unit), g_recv.at[side, unit])
        for side, target in ((1, at_right), (2, at_left)):

            @pl.when(core == side - 1)
            def _():
                remote(
                    unit_at(side, core, unit), unit_at(3, core, unit),
                    relay_send.at[unit], g_recv.at[3, unit], target,
                ).start()

        to_sibling(1, unit).start()
        to_sibling(2, unit).start()

    def opposite(unit):
        arrived(unit_at(3, core, unit), g_recv.at[3, unit])
        to_sibling(3, unit).start()

    def transfer(unit):
        arrived(transit.at[unit], t_recv.at[unit])

        @pl.when(holder)
        def _():
            hand_over[unit].start()

        @pl.when(follower)
        def _():
            hand_on[unit].start()

    def move_on(unit):
        arrived(transit.at[2 + unit], t_recv.at[2 + unit])
        onward[unit].start()

    def own_arrived(unit):
        arrived(unit_at(0, core, unit), g_recv.at[0, unit])

    bits_in.wait()

    def to_sign(group, carry):
        band = pl.ds(pl.multiple_of(group * BAND, BAND), BAND)
        sbuf[0, band, :] = (2 * sraw[band, :] - 1).astype(jnp.float32).astype(jnp.bfloat16)
        return carry

    lax.fori_loop(0, units // BAND, to_sign, 0)

    send_s = remote(sbuf.at[0], sbuf.at[1], s_send, s_recv, at_far)
    for copy in picks_in:
        copy.wait()
    sampled, features = picks[0], picks[1]
    group = jnp.zeros_like(sampled)
    for num in range(1, 16):
        group = group + (sampled >= num * units).astype(jnp.int32)
    block, col = features // 512, features % 512
    upper = bit_parity(jnp.bitwise_and(block, 6), 3)
    spot = (upper * 4 + col // LANES) * units + sampled - group * units
    ahead_of = (lax.broadcasted_iota(jnp.int32, (8, LANES), 1) // 16 + 8 - lax.broadcasted_iota(jnp.int32, (8, LANES), 0)) % 8
    for tile in range(PIECES):
        straight = spot[tile * 8:(tile + 1) * 8]
        turned = straight
        for d in range(1, 8):
            turned = jnp.where(ahead_of == d, pltpu.roll(pltpu.roll(straight, 8 - d, 0), 16 * d, 1), turned)
        for part in range(4):
            spots[tile * 4 + part] = turned[2 * part:2 * part + 2]
    sign = bit_parity(jnp.bitwise_and(group, wide), 4) + bit_parity(jnp.bitwise_and(block, narrow), 3)
    codes[...] = col % LANES + LANES * (sign % 2)

    lane_bits = lax.broadcasted_iota(jnp.int32, (8, LANES), 1) + LANES

    def weigh(first_tile, last_tile):
        def some(num, code):
            for inner in range(16):
                odd = jnp.bitwise_and(jnp.broadcast_to(code[:, inner:inner + 1], (8, LANES)), lane_bits)
                odd = jnp.bitwise_and(lax.population_count(odd), 1)
                weights[num // 8, num % 8 * 16 + inner] = jnp.where(odd == 1, -1.0, 1.0).astype(jnp.float32)
            code = pltpu.roll(code, LANES - 16, 1)
            after = jnp.minimum(num // 8 + 1, PIECES - 1)
            return jnp.where(num % 8 == 7, codes[pl.ds(pl.multiple_of(after * 8, 8), 8), :], code)

        lax.fori_loop(first_tile * 8, last_tile * 8, some, codes[first_tile * 8:(first_tile + 1) * 8, :])

    def spots_part(d, part):
        tile = lax.rem(piece + 1 + d, PIECES)
        return pltpu.make_async_copy(spots.at[tile * 4 + part], spots_smem.at[part], spot_sem.at[part])


    @pl.when(holder)
    def _():
        own_g.wait()
        spread(0)
        spread(1)

    transfer(0)

    @pl.when(holder)
    def _():
        own_arrived(2)
        spread(2)

    weigh(0, 1)
    transfer(1)
    for copy in by_z_pair[LEAD:]:
        copy.start()

    @pl.when(holder)
    def _():
        own_arrived(3)
        spread(3)
        move_on(0)

    @pl.when(follower)
    def _():
        own_arrived(0)
        spread(0)

    for num in BY_Z:
        pass_on(1, num)
    weigh(1, 2)

    @pl.when(holder)
    def _():
        move_on(1)

    @pl.when(follower)
    def _():
        own_arrived(1)
        spread(1)
        own_arrived(2)
        spread(2)

    send_s.start()
    around(0)
    weigh(2, 3)

    @pl.when(follower)
    def _():
        own_arrived(3)
        spread(3)

    around(1)
    weigh(3, 5)
    opposite(0)
    third = (len(by_y) + 2) // 3
    for num in by_y[:third]:
        pass_on(2, num)
    around(2)
    weigh(5, 6)
    opposite(1)
    around(3)
    weigh(6, 8)
    for num in by_y[third:2 * third]:
        pass_on(2, num)
    opposite(2)
    opposite(3)
    for num in by_y[2 * third:]:
        pass_on(2, num)

    total[...] = jnp.zeros_like(total)
    own_h.wait()
    for slot in range(4):
        for unit in range(UNITS):
            arrived(unit_at(slot, 1 - core, unit), core_recv.at[slot, unit])

    depth = acts.shape[0] // 2

    def step(num, carry):
        slot, half = div(num, 2), mod(num, 2)
        for which in (1, 2, 3):
            for one in range(CHUNKS):
                if not ((which == 1 and one in BY_Z) or (which == 2 and one in by_y)):

                    @pl.when(num == 2 * which + one // (CHUNKS // 2))
                    def _():
                        arrived(rows(which, one), h_recv.at[which - 1, one])

        from_y, from_z = mod(slot, 2), div(slot, 2)
        tokens = mod(y_bit + from_y, 2) * 2 + mod(z_lo + from_z, 2)
        ahead = mod(tokens - x + 4, 4)
        source = mod(ahead + div(ahead + 1, 2), 4)
        left = hbuf[slot, pl.ds(pl.multiple_of(half * depth, depth), depth), :]
        for part in range(2):
            total[part] += lax.dot_general(
                left, gbuf[source, half, part], (((0,), (0,)), ((), ())), preferred_element_type=jnp.float32
            )
        return carry

    for part in range(4):
        spots_part(0, part).start()
    lax.fori_loop(0, 8, step, 0)
    arrived(sbuf.at[1], s_recv)

    row_nums = lax.broadcasted_iota(jnp.int32, (BAND, 2 * BAND), 0)
    col_nums = lax.broadcasted_iota(jnp.int32, (BAND, 2 * BAND), 1)
    walsh = (1 - 2 * bit_parity(jnp.bitwise_and(row_nums, col_nums), 7)).astype(jnp.float32).astype(jnp.bfloat16)

    def mix(group, carry):
        band = pl.ds(pl.multiple_of(group * BAND, BAND), BAND)
        values = []
        for part in range(2):
            flipped = total[part, band, :] * sbuf[part, band, :].astype(jnp.float32)
            high = flipped.astype(jnp.bfloat16)
            low = (flipped - high.astype(jnp.float32)).astype(jnp.bfloat16)
            both = jnp.concatenate([high, low], axis=0)
            mixed = jnp.dot(walsh, both, preferred_element_type=jnp.float32)
            values += [mixed[:, k * LANES:(k + 1) * LANES] for k in range(4)]
        for stride in (1, 2, 4):
            values = [
                values[k - stride] - values[k] if k & stride else values[k] + values[k + stride]
                for k in range(8)
            ]
        for k in range(8):
            table[pl.ds(pl.multiple_of(k * units + group * BAND, BAND), BAND), :] = values[k]
        return carry

    lax.fori_loop(0, units // BAND, mix, 0)

    lane_nums = lax.broadcasted_iota(jnp.int32, (8, LANES), 1)
    sub_nums = lax.broadcasted_iota(jnp.int32, (8, LANES), 0)

    def pick(d, carry):
        tile = lax.rem(piece + 1 + d, PIECES)
        found = jnp.zeros((8, LANES), jnp.float32)
        for part in range(4):
            spots_part(d, part).wait()
            for num in (2 * part, 2 * part + 1):
                for inner in range(16):
                    for sub in range(8):
                        spot = spots_smem[part, num % 2, sub * 16 + inner]
                        row = jnp.broadcast_to(table[pl.ds(spot, 1), :], (8, LANES))
                        taken = row if sub == 0 else jnp.where(sub_nums == sub, row, taken)
                    lane = num * 16 + inner
                    value = jnp.sum(taken * weights[tile, lane], axis=1, keepdims=True)
                    found = jnp.where(lane_nums == lane, value, found)

            @pl.when(d < PIECES - 1)
            def _():
                spots_part(d + 1, part).start()

            if part == 0:
                for num in range(1, PIECES):

                    @pl.when(d == num)
                    def _():
                        ones[num - 1].start()

        terms[d] = found
        return carry

    ones = [
        remote(terms.at[d], first.at[d], send1.at[d], recv1.at[d], across[d]) for d in range(PIECES - 1)
    ]
    lax.fori_loop(0, PIECES, pick, 0)
    value = terms[PIECES - 1]
    for d, copy in enumerate(ones):
        copy.wait_recv()
        value = value + first[d]
    second[member] = value
    twos = [
        remote(second.at[member], second.at[member], send2.at[d], recv2.at[d], along[d]) for d in range(SPREAD - 1)
    ]
    for copy in twos:
        copy.start()
    for d in range(SPREAD - 1):
        source = second.at[mod(member + SPREAD - 1 - d, SPREAD)]
        remote(source, source, send2.at[d], recv2.at[d], along[d]).wait_recv()
    scale = 1.0 / math.sqrt(float(SEQ) * SEQ * 4096)
    for example in range(2):
        parts = [second[8 * hi + 4 * example + num] for hi in range(2) for num in range(4)]
        while len(parts) > 1:
            parts = [parts[k] + parts[k + 1] for k in range(0, len(parts), 2)]
        own[example] = parts[0] * scale
    for example in range(2):
        out[example, piece] = own[example]
    threes = [
        remote(own, out.at[:, piece], send3.at[d], recv3.at[d], across[d]) for d in range(PIECES - 1)
    ]
    for copy in threes:
        copy.start()
    for d in range(PIECES - 1):
        source = out.at[:, mod(piece + PIECES - 1 - d, PIECES)]
        remote(own, source, send3.at[d], recv3.at[d], across[d]).wait_recv()

    for copy in pending + ones + twos + threes:
        copy.wait_send()
    send_s.wait_send()
    for unit in range(UNITS):
        remote(
            unit_at(1, core, unit), unit_at(3, core, unit), relay_send.at[unit], g_recv.at[3, unit], at_core
        ).wait_send()

    for copy in cross + to_far + hand_on:
        copy.wait_send()


def shards(hidden, out_grad, sign_bits, pick_rows, pick_cols):
    units, features = sign_bits.shape
    tokens = hidden.shape[0]
    part_tokens = out_grad.shape[0]
    dma = pltpu.SemaphoreType.DMA
    tile = (8, LANES)
    hbm, vmem = pl.BlockSpec(memory_space=pltpu.HBM), pl.BlockSpec(memory_space=pltpu.VMEM)
    sums = pl.pallas_call(
        sketch_kernel,
        out_shape=jax.ShapeDtypeStruct((2, PIECES) + tile, jnp.float32),
        in_specs=[hbm] * 5,
        out_specs=vmem,
        scratch_shapes=[
            pltpu.VMEM((2, PIECES * 8, LANES), jnp.int32),
            pltpu.VMEM((4, tokens, units), jnp.bfloat16),
            pltpu.VMEM((4, 2, 2, part_tokens, features), jnp.bfloat16),
            pltpu.VMEM((UNITS, part_tokens // 2, features), jnp.bfloat16),
            pltpu.VMEM((units, features), jnp.int32),
            pltpu.VMEM((2, units, features), jnp.bfloat16),
            pltpu.VMEM((2, units, features), jnp.float32),
            pltpu.VMEM((8 * units, LANES), jnp.float32),
            pltpu.VMEM((PIECES * 4, 2, LANES), jnp.int32),
            pltpu.VMEM((PIECES * 8, LANES), jnp.int32),
            pltpu.VMEM((PIECES, LANES) + tile, jnp.float32),
            pltpu.SMEM((4, 2, LANES), jnp.int32),
            pltpu.VMEM((PIECES,) + tile, jnp.float32),
            pltpu.VMEM((PIECES - 1,) + tile, jnp.float32),
            pltpu.VMEM((SPREAD,) + tile, jnp.float32),
            pltpu.VMEM((2,) + tile, jnp.float32),
            dma((5,)), dma((4,)), dma((2 * CHUNKS,)), dma((2 * CHUNKS,)), dma((3, CHUNKS)), dma((2,)), dma((2,)), dma((2,)), dma((UNITS,)), dma((2, UNITS)),
            dma((UNITS,)), dma((4, UNITS)), dma((4, UNITS)), dma((4, UNITS)), dma, dma,
            dma((PIECES - 1,)), dma((PIECES - 1,)), dma((SPREAD - 1,)), dma((SPREAD - 1,)),
            dma((PIECES - 1,)), dma((PIECES - 1,)),
        ],
        compiler_params=pltpu.CompilerParams(
            collective_id=0, has_side_effects=True, vmem_limit_bytes=62 * 1024 * 1024
        ),
        name="sketch",
    )(hidden, out_grad, sign_bits, pick_rows.reshape(-1, LANES), pick_cols.reshape(-1, LANES))
    return sums.reshape(2, -1)


def solution(mesh):
    placed = (P("narrow", "wide"), P("wide", "narrow"), P("wide", "narrow"), P(), P())
    return jax.shard_map(shards, mesh=mesh, in_specs=placed, out_specs=P(), check_vma=False)
```

```python
import math

import jax
import jax.numpy as jnp
from jax import lax
from jax.experimental import pallas as pl
from jax.experimental.pallas import tpu as pltpu
from jax.sharding import PartitionSpec as P

SEQ = 2048
BAND = 128
LANES = 128
PIECES = 8
SPREAD = 16
UNITS = 4
CHUNKS = 8
BY_Z = (5, 6, 7)
LEAD = 2
MESH = pl.DeviceIdType.MESH


def bit_parity(value, count):
    total = jnp.zeros_like(value)
    for bit_num in range(count):
        total = total + jnp.bitwise_and(jnp.right_shift(value, bit_num), 1)
    return jnp.bitwise_and(total, 1)


def div(value, by):
    return lax.div(value, jnp.int32(by))


def mod(value, by):
    return lax.rem(value, jnp.int32(by))


def place():
    wide, narrow = lax.axis_index("wide"), lax.axis_index("narrow")
    return div(wide, 8), mod(div(wide, 2), 4), mod(wide, 2), div(narrow, 2), mod(narrow, 2)


def device(z_hi, x, core, y, z_lo):
    return (z_hi * 8 + x * 2 + core, y * 2 + z_lo)


def sketch_kernel(
    acts, grads, sign_bits, pick_rows, pick_cols, out,
    picks, hbuf, gbuf, transit, sraw, sbuf, total, table, spots, codes, weights, spots_smem, terms, first, second, own,
    local_sem, spot_sem, hy_send, hz_send, h_recv, init_send, far_send, t_send, t_recv, x_send, relay_send, g_recv,
    core_send, core_recv, s_send, s_recv, send1, recv1, send2, recv2, send3, recv3,
):
    wide, narrow = lax.axis_index("wide"), lax.axis_index("narrow")
    z_hi, x, core, y, z_lo = place()
    units = sraw.shape[0]
    y_bit, upper_y = mod(y, 2), div(y, 2)
    y_pair = y + 1 - 2 * y_bit
    at_y = device(z_hi, x, core, y_pair, z_lo)
    at_z = device(z_hi, x, core, y, 1 - z_lo)
    at_far = device(z_hi, x, core, 3 - y, z_lo)
    at_cross = device(1 - z_hi, x, core, y, 1 - z_lo)
    at_right = device(z_hi, mod(x + 1, 4), core, y, z_lo)
    at_left = device(z_hi, mod(x + 3, 4), core, y, z_lo)
    at_core = device(z_hi, x, 1 - core, y, z_lo)
    holder = upper_y == z_hi
    chunk = acts.shape[0] // CHUNKS

    piece = x * 2 + core
    member = (z_hi * 4 + y) * 2 + z_lo
    ways = ((2, 0), (2, 1), (1, 0), (1, 1), (3, 0), (3, 1), (0, 1))
    pieces = [mod(x + dx, 4) * 2 + mod(core + dc, 2) for dx, dc in ways]
    sources = [mod(x + 4 - dx, 4) * 2 + mod(core + dc, 2) for dx, dc in ways]
    members = [mod(member + d, SPREAD) for d in range(1, SPREAD)]
    across = [(z_hi * 8 + t, narrow) for t in pieces]
    along = [(div(g, 8) * 8 + piece, mod(g, 8)) for g in members]

    barrier = pltpu.get_barrier_semaphore()
    for peer in across + along:
        pl.semaphore_signal(barrier, inc=1, device_id=peer, device_id_type=MESH)
    bits_in = pltpu.make_async_copy(sign_bits, sraw, local_sem.at[1])
    bits_in.start()
    own_h = pltpu.make_async_copy(acts, hbuf.at[0], local_sem.at[0])
    own_h.start()
    picks_in = [
        pltpu.make_async_copy(source, picks.at[num], local_sem.at[3 + num])
        for num, source in enumerate((pick_rows, pick_cols))
    ]
    for copy in picks_in:
        copy.start()
    pl.semaphore_wait(barrier, len(across + along))

    def remote(src, dst, send, recv, target):
        return pltpu.make_async_remote_copy(
            src_ref=src, dst_ref=dst, send_sem=send, recv_sem=recv, device_id=target, device_id_type=MESH
        )

    def arrived(ref, recv):
        remote(ref, ref, s_send, recv, at_core).wait_recv()

    own_g = pltpu.make_async_copy(grads, gbuf.at[0, core, 0], local_sem.at[2])
    few = grads.shape[0] // 2

    def piece_of(ref, unit):
        return ref.at[pl.ds(unit % 2 * few, few)]

    def unit_at(slot, half, unit):
        return gbuf.at[slot, half, unit // 2, pl.ds(unit % 2 * few, few)]

    follower = jnp.logical_not(holder)
    cross = [
        remote(piece_of(grads, unit), transit.at[unit], init_send.at[unit], t_recv.at[unit], at_cross)
        for unit in range(2)
    ]
    to_far = [
        remote(piece_of(grads, unit), unit_at(0, core, 2 + unit), far_send.at[unit], g_recv.at[0, 2 + unit], at_far)
        for unit in range(2)
    ]
    hand_on = [
        remote(transit.at[unit], unit_at(0, core, unit), t_send.at[unit], g_recv.at[0, unit], at_z)
        for unit in range(2)
    ]
    hand_over = [
        remote(transit.at[unit], transit.at[2 + unit], t_send.at[unit], t_recv.at[2 + unit], at_z)
        for unit in range(2)
    ]
    onward = [
        remote(
            transit.at[2 + unit], unit_at(0, core, 2 + unit), far_send.at[unit], g_recv.at[0, 2 + unit], at_far
        )
        for unit in range(2)
    ]
    for copy in cross:
        copy.start()

    @pl.when(holder)
    def _():
        own_g.start()

    @pl.when(follower)
    def _():
        for copy in to_far:
            copy.start()

    pending = []
    by_y = tuple(num for num in range(CHUNKS) if num not in BY_Z)
    def activations(slot, num):
        sends, target = ((hy_send, at_y), (hz_send, at_z))[slot - 1]
        copy = remote(
            acts.at[pl.ds(num * chunk, chunk)], hbuf.at[slot, pl.ds(num * chunk, chunk)],
            sends.at[num], h_recv.at[slot - 1, num], target,
        )
        pending.append(copy)
        return copy

    by_z_pair = [activations(2, num) for num in by_y + BY_Z]
    for copy in by_z_pair[:LEAD]:
        copy.start()
    for num in BY_Z + by_y:
        activations(1, num).start()

    def rows(slot, num):
        return hbuf.at[slot, pl.ds(num * chunk, chunk)]

    def pass_on(slot, num):
        arrived(rows(slot, num), h_recv.at[slot - 1, num])
        sends, target = ((hz_send, at_z), (hy_send, at_y))[slot - 1]
        copy = remote(rows(slot, num), rows(3, num), sends.at[CHUNKS + num], h_recv.at[2, num], target)
        copy.start()
        pending.append(copy)

    def to_sibling(slot, unit):
        block = unit_at(slot, core, unit)
        copy = remote(block, block, core_send.at[slot, unit], core_recv.at[slot, unit], at_core)
        pending.append(copy)
        return copy

    spreads = [
        [
            remote(
                unit_at(0, core, unit), unit_at(side, core, unit), x_send.at[side - 1, unit],
                g_recv.at[side, unit], target,
            )
            for side, target in ((1, at_right), (2, at_left))
        ]
        for unit in range(UNITS)
    ]
    for copies in spreads:
        pending.extend(copies)
    own_siblings = [to_sibling(0, unit) for unit in range(UNITS)]

    def spread(unit):
        for copy in spreads[unit]:
            copy.start()
        own_siblings[unit].start()

    def around(unit):
        for side in (1, 2):
            arrived(unit_at(side, core, unit), g_recv.at[side, unit])
        for side, target in ((1, at_right), (2, at_left)):

            @pl.when(core == side - 1)
            def _():
                remote(
                    unit_at(side, core, unit), unit_at(3, core, unit),
                    relay_send.at[unit], g_recv.at[3, unit], target,
                ).start()

        to_sibling(1, unit).start()
        to_sibling(2, unit).start()

    def opposite(unit):
        arrived(unit_at(3, core, unit), g_recv.at[3, unit])
        to_sibling(3, unit).start()

    def transfer(unit):
        arrived(transit.at[unit], t_recv.at[unit])

        @pl.when(holder)
        def _():
            hand_over[unit].start()

        @pl.when(follower)
        def _():
            hand_on[unit].start()

    def move_on(unit):
        arrived(transit.at[2 + unit], t_recv.at[2 + unit])
        onward[unit].start()

    def own_arrived(unit):
        arrived(unit_at(0, core, unit), g_recv.at[0, unit])

    bits_in.wait()

    def to_sign(group, carry):
        band = pl.ds(pl.multiple_of(group * BAND, BAND), BAND)
        sbuf[0, band, :] = (2 * sraw[band, :] - 1).astype(jnp.float32).astype(jnp.bfloat16)
        return carry

    lax.fori_loop(0, units // BAND, to_sign, 0)

    send_s = remote(sbuf.at[0], sbuf.at[1], s_send, s_recv, at_far)
    for copy in picks_in:
        copy.wait()
    sampled, features = picks[0], picks[1]
    group = jnp.zeros_like(sampled)
    for num in range(1, 16):
        group = group + (sampled >= num * units).astype(jnp.int32)
    block, col = features // 512, features % 512
    upper = bit_parity(jnp.bitwise_and(block, 6), 3)
    spot = (upper * 4 + col // LANES) * units + sampled - group * units
    ahead_of = (lax.broadcasted_iota(jnp.int32, (8, LANES), 1) // 16 + 8 - lax.broadcasted_iota(jnp.int32, (8, LANES), 0)) % 8
    for tile in range(PIECES):
        straight = spot[tile * 8:(tile + 1) * 8]
        turned = straight
        for d in range(1, 8):
            turned = jnp.where(ahead_of == d, pltpu.roll(pltpu.roll(straight, 8 - d, 0), 16 * d, 1), turned)
        for part in range(2):
            spots[tile * 2 + part] = turned[4 * part:4 * part + 4]
    sign = bit_parity(jnp.bitwise_and(group, wide), 4) + bit_parity(jnp.bitwise_and(block, narrow), 3)
    codes[...] = col % LANES + LANES * (sign % 2)

    lane_bits = lax.broadcasted_iota(jnp.int32, (8, LANES), 1) + LANES

    def weigh(first_tile, last_tile):
        def some(num, code):
            for inner in range(16):
                odd = jnp.bitwise_and(jnp.broadcast_to(code[:, inner:inner + 1], (8, LANES)), lane_bits)
                odd = jnp.bitwise_and(lax.population_count(odd), 1)
                weights[num // 8, num % 8 * 16 + inner] = jnp.where(odd == 1, -1.0, 1.0).astype(jnp.float32)
            code = pltpu.roll(code, LANES - 16, 1)
            after = jnp.minimum(num // 8 + 1, PIECES - 1)
            return jnp.where(num % 8 == 7, codes[pl.ds(pl.multiple_of(after * 8, 8), 8), :], code)

        lax.fori_loop(first_tile * 8, last_tile * 8, some, codes[first_tile * 8:(first_tile + 1) * 8, :])

    def turn(d):
        pair = div(d, 2)
        ahead = 2 + 3 * pair + 3 * div(pair, 2) + 2 * div(pair, 3)
        return mod(x + ahead, 4) * 2 + mod(core + d + div(d, 6), 2)

    def spots_part(d, part, buffer):
        tile = turn(d)
        return pltpu.make_async_copy(spots.at[tile * 2 + part], spots_smem.at[2 * buffer + part], spot_sem.at[2 * buffer + part])


    @pl.when(holder)
    def _():
        own_g.wait()
        spread(0)
        spread(1)

    transfer(0)

    @pl.when(holder)
    def _():
        own_arrived(2)
        spread(2)

    weigh(0, 1)
    transfer(1)
    for copy in by_z_pair[LEAD:]:
        copy.start()

    @pl.when(holder)
    def _():
        own_arrived(3)
        spread(3)
        move_on(0)

    @pl.when(follower)
    def _():
        own_arrived(0)
        spread(0)

    for num in BY_Z:
        pass_on(1, num)
    weigh(1, 2)

    @pl.when(holder)
    def _():
        move_on(1)

    @pl.when(follower)
    def _():
        own_arrived(1)
        spread(1)
        own_arrived(2)
        spread(2)

    send_s.start()
    around(0)
    weigh(2, 3)

    @pl.when(follower)
    def _():
        own_arrived(3)
        spread(3)

    around(1)
    weigh(3, 5)
    opposite(0)
    third = (len(by_y) + 2) // 3
    for num in by_y[:third]:
        pass_on(2, num)
    around(2)
    weigh(5, 6)
    opposite(1)
    around(3)
    weigh(6, 8)
    for num in by_y[third:2 * third]:
        pass_on(2, num)
    opposite(2)
    opposite(3)
    for num in by_y[2 * third:]:
        pass_on(2, num)

    total[...] = jnp.zeros_like(total)
    own_h.wait()
    for slot in range(4):
        for unit in range(UNITS):
            arrived(unit_at(slot, 1 - core, unit), core_recv.at[slot, unit])

    depth = acts.shape[0] // 2

    def step(num, carry):
        slot, half = div(num, 2), mod(num, 2)
        for which in (1, 2, 3):
            for one in range(CHUNKS):
                if not ((which == 1 and one in BY_Z) or (which == 2 and one in by_y)):

                    @pl.when(num == 2 * which + one // (CHUNKS // 2))
                    def _():
                        arrived(rows(which, one), h_recv.at[which - 1, one])

        from_y, from_z = mod(slot, 2), div(slot, 2)
        tokens = mod(y_bit + from_y, 2) * 2 + mod(z_lo + from_z, 2)
        ahead = mod(tokens - x + 4, 4)
        source = mod(ahead + div(ahead + 1, 2), 4)
        left = hbuf[slot, pl.ds(pl.multiple_of(half * depth, depth), depth), :]
        for part in range(2):
            total[part] += lax.dot_general(
                left, gbuf[source, half, part], (((0,), (0,)), ((), ())), preferred_element_type=jnp.float32
            )
        return carry

    for part in range(2):
        spots_part(0, part, 0).start()
        spots_part(1, part, 1).start()
    lax.fori_loop(0, 8, step, 0)
    arrived(sbuf.at[1], s_recv)

    row_nums = lax.broadcasted_iota(jnp.int32, (BAND, 2 * BAND), 0)
    col_nums = lax.broadcasted_iota(jnp.int32, (BAND, 2 * BAND), 1)
    walsh = (1 - 2 * bit_parity(jnp.bitwise_and(row_nums, col_nums), 7)).astype(jnp.float32).astype(jnp.bfloat16)

    def mix(group, carry):
        band = pl.ds(pl.multiple_of(group * BAND, BAND), BAND)
        values = []
        for part in range(2):
            value, flip = total[part, band, :], sbuf[part, band, :]
            high = value.astype(jnp.bfloat16)
            low = (value - high.astype(jnp.float32)).astype(jnp.bfloat16)
            both = jnp.concatenate([high * flip, low * flip], axis=0)
            mixed = jnp.dot(walsh, both, preferred_element_type=jnp.float32)
            values += [mixed[:, k * LANES:(k + 1) * LANES] for k in range(4)]
        for stride in (1, 2, 4):
            values = [
                values[k - stride] - values[k] if k & stride else values[k] + values[k + stride]
                for k in range(8)
            ]
        for k in range(8):
            table[pl.ds(pl.multiple_of(k * units + group * BAND, BAND), BAND), :] = values[k]
        return carry

    lax.fori_loop(0, units // BAND, mix, 0)

    lane_nums = lax.broadcasted_iota(jnp.int32, (8, LANES), 1)
    sub_nums = lax.broadcasted_iota(jnp.int32, (8, LANES), 0)

    def pick(d, buffer):
        tile = turn(d)
        found = jnp.zeros((8, LANES), jnp.float32)
        for part in range(2):
            spots_part(d, part, buffer).wait()
            for num in range(4 * part, 4 * part + 4):
                for inner in range(16):
                    for sub in range(8):
                        spot = spots_smem[2 * buffer + part, num % 4, sub * 16 + inner]
                        row = jnp.broadcast_to(table[pl.ds(spot, 1), :], (8, LANES))
                        taken = row if sub == 0 else jnp.where(sub_nums == sub, row, taken)
                    lane = num * 16 + inner
                    value = jnp.sum(taken * weights[tile, lane], axis=1, keepdims=True)
                    found = jnp.where(lane_nums == lane, value, found)

            @pl.when(d < PIECES - 2)
            def _():
                spots_part(d + 2, part, buffer).start()

            if part == 0:
                for num in range(1, PIECES):

                    @pl.when(d == num)
                    def _():
                        ones[num - 1].start()

        terms[d] = found

    def pick_two(num, carry):
        pick(2 * num, 0)
        pick(2 * num + 1, 1)
        return carry

    ones = [
        remote(terms.at[d], first.at[d], send1.at[d], recv1.at[d], across[d]) for d in range(PIECES - 1)
    ]
    lax.fori_loop(0, PIECES // 2, pick_two, 0)
    value = terms[PIECES - 1]
    for d, copy in enumerate(ones):
        copy.wait_recv()
        value = value + first[d]
    second[member] = value
    twos = [
        remote(second.at[member], second.at[member], send2.at[d], recv2.at[d], along[d]) for d in range(SPREAD - 1)
    ]
    for copy in twos:
        copy.start()
    for copy in pending:
        copy.wait_send()
    send_s.wait_send()
    for unit in range(UNITS):
        remote(
            unit_at(1, core, unit), unit_at(3, core, unit), relay_send.at[unit], g_recv.at[3, unit], at_core
        ).wait_send()

    for copy in cross + to_far + hand_on:
        copy.wait_send()
    for d in range(SPREAD - 1):
        source = second.at[mod(member + SPREAD - 1 - d, SPREAD)]
        remote(source, source, send2.at[d], recv2.at[d], along[d]).wait_recv()
    scale = 1.0 / math.sqrt(float(SEQ) * SEQ * 4096)
    for example in range(2):
        parts = [second[8 * hi + 4 * example + num] for hi in range(2) for num in range(4)]
        while len(parts) > 1:
            parts = [parts[k] + parts[k + 1] for k in range(0, len(parts), 2)]
        own[example] = parts[0] * scale
    for example in range(2):
        out[example, piece] = own[example]
    threes = [
        remote(own, out.at[:, piece], send3.at[d], recv3.at[d], across[d]) for d in range(PIECES - 1)
    ]
    for copy in threes:
        copy.start()
    for d in range(PIECES - 1):
        source = out.at[:, sources[d]]
        remote(own, source, send3.at[d], recv3.at[d], across[d]).wait_recv()

    for copy in ones + twos + threes:
        copy.wait_send()


def shards(hidden, out_grad, sign_bits, pick_rows, pick_cols):
    units, features = sign_bits.shape
    tokens = hidden.shape[0]
    part_tokens = out_grad.shape[0]
    dma = pltpu.SemaphoreType.DMA
    tile = (8, LANES)
    hbm, vmem = pl.BlockSpec(memory_space=pltpu.HBM), pl.BlockSpec(memory_space=pltpu.VMEM)
    sums = pl.pallas_call(
        sketch_kernel,
        out_shape=jax.ShapeDtypeStruct((2, PIECES) + tile, jnp.float32),
        in_specs=[hbm] * 5,
        out_specs=vmem,
        scratch_shapes=[
            pltpu.VMEM((2, PIECES * 8, LANES), jnp.int32),
            pltpu.VMEM((4, tokens, units), jnp.bfloat16),
            pltpu.VMEM((4, 2, 2, part_tokens, features), jnp.bfloat16),
            pltpu.VMEM((UNITS, part_tokens // 2, features), jnp.bfloat16),
            pltpu.VMEM((units, features), jnp.int32),
            pltpu.VMEM((2, units, features), jnp.bfloat16),
            pltpu.VMEM((2, units, features), jnp.float32),
            pltpu.VMEM((8 * units, LANES), jnp.float32),
            pltpu.VMEM((PIECES * 2, 4, LANES), jnp.int32),
            pltpu.VMEM((PIECES * 8, LANES), jnp.int32),
            pltpu.VMEM((PIECES, LANES) + tile, jnp.float32),
            pltpu.SMEM((4, 4, LANES), jnp.int32),
            pltpu.VMEM((PIECES,) + tile, jnp.float32),
            pltpu.VMEM((PIECES - 1,) + tile, jnp.float32),
            pltpu.VMEM((SPREAD,) + tile, jnp.float32),
            pltpu.VMEM((2,) + tile, jnp.float32),
            dma((5,)), dma((4,)), dma((2 * CHUNKS,)), dma((2 * CHUNKS,)), dma((3, CHUNKS)), dma((2,)), dma((2,)), dma((2,)), dma((UNITS,)), dma((2, UNITS)),
            dma((UNITS,)), dma((4, UNITS)), dma((4, UNITS)), dma((4, UNITS)), dma, dma,
            dma((PIECES - 1,)), dma((PIECES - 1,)), dma((SPREAD - 1,)), dma((SPREAD - 1,)),
            dma((PIECES - 1,)), dma((PIECES - 1,)),
        ],
        compiler_params=pltpu.CompilerParams(
            collective_id=0, has_side_effects=True, vmem_limit_bytes=62 * 1024 * 1024
        ),
        name="sketch",
    )(hidden, out_grad, sign_bits, pick_rows.reshape(-1, LANES), pick_cols.reshape(-1, LANES))
    return sums.reshape(2, -1)


def solution(mesh):
    placed = (P("narrow", "wide"), P("wide", "narrow"), P("wide", "narrow"), P(), P())
    return jax.shard_map(shards, mesh=mesh, in_specs=placed, out_specs=P(), check_vma=False)
```

```python
import math

import jax
import jax.numpy as jnp
from jax import lax
from jax.experimental import pallas as pl
from jax.experimental.pallas import tpu as pltpu
from jax.sharding import PartitionSpec as P

SEQ = 2048
BAND = 128
LANES = 128
PIECES = 8
SPREAD = 16
UNITS = 4
CHUNKS = 8
BY_Z = (5, 6, 7)
LEAD = 2
MESH = pl.DeviceIdType.MESH


def bit_parity(value, count):
    total = jnp.zeros_like(value)
    for bit_num in range(count):
        total = total + jnp.bitwise_and(jnp.right_shift(value, bit_num), 1)
    return jnp.bitwise_and(total, 1)


def div(value, by):
    return lax.div(value, jnp.int32(by))


def mod(value, by):
    return lax.rem(value, jnp.int32(by))


def place():
    wide, narrow = lax.axis_index("wide"), lax.axis_index("narrow")
    return div(wide, 8), mod(div(wide, 2), 4), mod(wide, 2), div(narrow, 2), mod(narrow, 2)


def device(z_hi, x, core, y, z_lo):
    return (z_hi * 8 + x * 2 + core, y * 2 + z_lo)


def sketch_kernel(
    acts, grads, sign_bits, pick_rows, pick_cols, out,
    picks, hbuf, gbuf, transit, sraw, sbuf, total, table, spots, codes, weights, spots_smem, terms, first, second, own,
    local_sem, spot_sem, hy_send, hz_send, h_recv, init_send, far_send, t_send, t_recv, x_send, relay_send, g_recv,
    core_send, core_recv, s_send, s_recv, send1, recv1, send2, recv2, send3, recv3,
):
    wide, narrow = lax.axis_index("wide"), lax.axis_index("narrow")
    z_hi, x, core, y, z_lo = place()
    units = sraw.shape[0]
    y_bit, upper_y = mod(y, 2), div(y, 2)
    y_pair = y + 1 - 2 * y_bit
    at_y = device(z_hi, x, core, y_pair, z_lo)
    at_z = device(z_hi, x, core, y, 1 - z_lo)
    at_far = device(z_hi, x, core, 3 - y, z_lo)
    at_cross = device(1 - z_hi, x, core, y, 1 - z_lo)
    at_right = device(z_hi, mod(x + 1, 4), core, y, z_lo)
    at_left = device(z_hi, mod(x + 3, 4), core, y, z_lo)
    at_core = device(z_hi, x, 1 - core, y, z_lo)
    holder = upper_y == z_hi
    chunk = acts.shape[0] // CHUNKS

    piece = x * 2 + core
    member = (z_hi * 4 + y) * 2 + z_lo
    ways = ((2, 0), (2, 1), (1, 0), (1, 1), (3, 0), (3, 1), (0, 1))
    pieces = [mod(x + dx, 4) * 2 + mod(core + dc, 2) for dx, dc in ways]
    sources = [mod(x + 4 - dx, 4) * 2 + mod(core + dc, 2) for dx, dc in ways]
    members = [mod(member + d, SPREAD) for d in range(1, SPREAD)]
    across = [(z_hi * 8 + t, narrow) for t in pieces]
    along = [(div(g, 8) * 8 + piece, mod(g, 8)) for g in members]

    barrier = pltpu.get_barrier_semaphore()
    for peer in across + along:
        pl.semaphore_signal(barrier, inc=1, device_id=peer, device_id_type=MESH)
    bits_in = pltpu.make_async_copy(sign_bits, sraw, local_sem.at[1])
    bits_in.start()
    own_h = pltpu.make_async_copy(acts, hbuf.at[0], local_sem.at[0])
    own_h.start()
    picks_in = [
        pltpu.make_async_copy(source, picks.at[num], local_sem.at[3 + num])
        for num, source in enumerate((pick_rows, pick_cols))
    ]
    for copy in picks_in:
        copy.start()
    pl.semaphore_wait(barrier, len(across + along))

    def remote(src, dst, send, recv, target):
        return pltpu.make_async_remote_copy(
            src_ref=src, dst_ref=dst, send_sem=send, recv_sem=recv, device_id=target, device_id_type=MESH
        )

    def arrived(ref, recv):
        remote(ref, ref, s_send, recv, at_core).wait_recv()

    own_g = pltpu.make_async_copy(grads, gbuf.at[0, core, 0], local_sem.at[2])
    few = grads.shape[0] // 2

    def piece_of(ref, unit):
        return ref.at[pl.ds(unit % 2 * few, few)]

    def unit_at(slot, half, unit):
        return gbuf.at[slot, half, unit // 2, pl.ds(unit % 2 * few, few)]

    follower = jnp.logical_not(holder)
    cross = [
        remote(piece_of(grads, unit), transit.at[unit], init_send.at[unit], t_recv.at[unit], at_cross)
        for unit in range(2)
    ]
    to_far = [
        remote(piece_of(grads, unit), unit_at(0, core, 2 + unit), far_send.at[unit], g_recv.at[0, 2 + unit], at_far)
        for unit in range(2)
    ]
    hand_on = [
        remote(transit.at[unit], unit_at(0, core, unit), t_send.at[unit], g_recv.at[0, unit], at_z)
        for unit in range(2)
    ]
    hand_over = [
        remote(transit.at[unit], transit.at[2 + unit], t_send.at[unit], t_recv.at[2 + unit], at_z)
        for unit in range(2)
    ]
    onward = [
        remote(
            transit.at[2 + unit], unit_at(0, core, 2 + unit), far_send.at[unit], g_recv.at[0, 2 + unit], at_far
        )
        for unit in range(2)
    ]
    for copy in cross:
        copy.start()

    @pl.when(holder)
    def _():
        own_g.start()

    @pl.when(follower)
    def _():
        for copy in to_far:
            copy.start()

    pending = []
    by_y = tuple(num for num in range(CHUNKS) if num not in BY_Z)
    def activations(slot, num):
        sends, target = ((hy_send, at_y), (hz_send, at_z))[slot - 1]
        copy = remote(
            acts.at[pl.ds(num * chunk, chunk)], hbuf.at[slot, pl.ds(num * chunk, chunk)],
            sends.at[num], h_recv.at[slot - 1, num], target,
        )
        pending.append(copy)
        return copy

    by_z_pair = [activations(2, num) for num in by_y + BY_Z]
    for copy in by_z_pair[:LEAD]:
        copy.start()
    for num in BY_Z + by_y:
        activations(1, num).start()

    def rows(slot, num):
        return hbuf.at[slot, pl.ds(num * chunk, chunk)]

    def pass_on(slot, num):
        arrived(rows(slot, num), h_recv.at[slot - 1, num])
        sends, target = ((hz_send, at_z), (hy_send, at_y))[slot - 1]
        copy = remote(rows(slot, num), rows(3, num), sends.at[CHUNKS + num], h_recv.at[2, num], target)
        copy.start()
        pending.append(copy)

    def to_sibling(slot, unit):
        block = unit_at(slot, core, unit)
        copy = remote(block, block, core_send.at[slot, unit], core_recv.at[slot, unit], at_core)
        pending.append(copy)
        return copy

    spreads = [
        [
            remote(
                unit_at(0, core, unit), unit_at(side, core, unit), x_send.at[side - 1, unit],
                g_recv.at[side, unit], target,
            )
            for side, target in ((1, at_right), (2, at_left))
        ]
        for unit in range(UNITS)
    ]
    for copies in spreads:
        pending.extend(copies)
    own_siblings = [to_sibling(0, unit) for unit in range(UNITS)]

    def spread(unit):
        for copy in spreads[unit]:
            copy.start()
        own_siblings[unit].start()

    def around(unit):
        for side in (1, 2):
            arrived(unit_at(side, core, unit), g_recv.at[side, unit])
        for side, target in ((1, at_right), (2, at_left)):

            @pl.when(core == side - 1)
            def _():
                remote(
                    unit_at(side, core, unit), unit_at(3, core, unit),
                    relay_send.at[unit], g_recv.at[3, unit], target,
                ).start()

        to_sibling(1, unit).start()
        to_sibling(2, unit).start()

    def opposite(unit):
        arrived(unit_at(3, core, unit), g_recv.at[3, unit])
        to_sibling(3, unit).start()

    def transfer(unit):
        arrived(transit.at[unit], t_recv.at[unit])

        @pl.when(holder)
        def _():
            hand_over[unit].start()

        @pl.when(follower)
        def _():
            hand_on[unit].start()

    def move_on(unit):
        arrived(transit.at[2 + unit], t_recv.at[2 + unit])
        onward[unit].start()

    def own_arrived(unit):
        arrived(unit_at(0, core, unit), g_recv.at[0, unit])

    bits_in.wait()

    def to_sign(group, carry):
        band = pl.ds(pl.multiple_of(group * BAND, BAND), BAND)
        sbuf[0, band, :] = (2 * sraw[band, :] - 1).astype(jnp.float32).astype(jnp.bfloat16)
        return carry

    lax.fori_loop(0, units // BAND, to_sign, 0)

    send_s = remote(sbuf.at[0], sbuf.at[1], s_send, s_recv, at_far)
    for copy in picks_in:
        copy.wait()
    sampled, features = picks[0], picks[1]
    group = jnp.zeros_like(sampled)
    for num in range(1, 16):
        group = group + (sampled >= num * units).astype(jnp.int32)
    block, col = features // 512, features % 512
    upper = bit_parity(jnp.bitwise_and(block, 6), 3)
    spot = (upper * 4 + col // LANES) * units + sampled - group * units
    ahead_of = (lax.broadcasted_iota(jnp.int32, (8, LANES), 1) // 16 + 8 - lax.broadcasted_iota(jnp.int32, (8, LANES), 0)) % 8
    for tile in range(PIECES):
        straight = spot[tile * 8:(tile + 1) * 8]
        turned = straight
        for d in range(1, 8):
            turned = jnp.where(ahead_of == d, pltpu.roll(pltpu.roll(straight, 8 - d, 0), 16 * d, 1), turned)
        for part in range(2):
            spots[tile * 2 + part] = turned[4 * part:4 * part + 4]
    sign = bit_parity(jnp.bitwise_and(group, wide), 4) + bit_parity(jnp.bitwise_and(block, narrow), 3)
    codes[...] = col % LANES + LANES * (sign % 2)

    lane_bits = lax.broadcasted_iota(jnp.int32, (8, LANES), 1) + LANES

    def weigh(first_tile, last_tile):
        def some(num, code):
            for inner in range(16):
                odd = jnp.bitwise_and(jnp.broadcast_to(code[:, inner:inner + 1], (8, LANES)), lane_bits)
                odd = jnp.bitwise_and(lax.population_count(odd), 1)
                weights[num // 8, num % 8 * 16 + inner] = jnp.where(odd == 1, -1.0, 1.0).astype(jnp.float32)
            code = pltpu.roll(code, LANES - 16, 1)
            after = jnp.minimum(num // 8 + 1, PIECES - 1)
            return jnp.where(num % 8 == 7, codes[pl.ds(pl.multiple_of(after * 8, 8), 8), :], code)

        lax.fori_loop(first_tile * 8, last_tile * 8, some, codes[first_tile * 8:(first_tile + 1) * 8, :])

    def turn(d):
        pair = div(d, 2)
        ahead = 2 + 3 * pair + 3 * div(pair, 2) + 2 * div(pair, 3)
        return mod(x + ahead, 4) * 2 + mod(core + d + div(d, 6), 2)

    def spots_part(d, part, buffer):
        tile = turn(d)
        return pltpu.make_async_copy(spots.at[tile * 2 + part], spots_smem.at[2 * buffer + part], spot_sem.at[2 * buffer + part])


    @pl.when(holder)
    def _():
        own_g.wait()
        spread(0)
        spread(1)

    transfer(0)

    @pl.when(holder)
    def _():
        own_arrived(2)
        spread(2)

    weigh(0, 1)
    transfer(1)
    for copy in by_z_pair[LEAD:]:
        copy.start()

    @pl.when(holder)
    def _():
        own_arrived(3)
        spread(3)
        move_on(0)

    @pl.when(follower)
    def _():
        own_arrived(0)
        spread(0)

    for num in BY_Z:
        pass_on(1, num)
    weigh(1, 2)

    @pl.when(holder)
    def _():
        move_on(1)

    @pl.when(follower)
    def _():
        own_arrived(1)
        spread(1)
        own_arrived(2)
        spread(2)

    send_s.start()
    around(0)
    weigh(2, 3)

    @pl.when(follower)
    def _():
        own_arrived(3)
        spread(3)

    around(1)
    weigh(3, 5)
    opposite(0)
    third = (len(by_y) + 2) // 3
    for num in by_y[:third]:
        pass_on(2, num)
    around(2)
    weigh(5, 6)
    opposite(1)
    around(3)
    weigh(6, 8)
    for num in by_y[third:2 * third]:
        pass_on(2, num)
    opposite(2)
    opposite(3)
    for num in by_y[2 * third:]:
        pass_on(2, num)

    total[...] = jnp.zeros_like(total)
    own_h.wait()
    for slot in range(4):
        for unit in range(UNITS):
            arrived(unit_at(slot, 1 - core, unit), core_recv.at[slot, unit])

    depth = acts.shape[0] // 2

    def step(num, carry):
        slot, half = div(num, 2), mod(num, 2)
        for which in (1, 2, 3):
            for one in range(CHUNKS):
                if not ((which == 1 and one in BY_Z) or (which == 2 and one in by_y)):

                    @pl.when(num == 2 * which + one // (CHUNKS // 2))
                    def _():
                        arrived(rows(which, one), h_recv.at[which - 1, one])

        from_y, from_z = mod(slot, 2), div(slot, 2)
        tokens = mod(y_bit + from_y, 2) * 2 + mod(z_lo + from_z, 2)
        ahead = mod(tokens - x + 4, 4)
        source = mod(ahead + div(ahead + 1, 2), 4)
        left = hbuf[slot, pl.ds(pl.multiple_of(half * depth, depth), depth), :]
        for part in range(2):
            total[part] += lax.dot_general(
                left, gbuf[source, half, part], (((0,), (0,)), ((), ())), preferred_element_type=jnp.float32
            )
        return carry

    for part in range(2):
        spots_part(0, part, 0).start()
        spots_part(1, part, 1).start()
    lax.fori_loop(0, 8, step, 0)
    arrived(sbuf.at[1], s_recv)

    row_nums = lax.broadcasted_iota(jnp.int32, (BAND, 2 * BAND), 0)
    col_nums = lax.broadcasted_iota(jnp.int32, (BAND, 2 * BAND), 1)
    walsh = (1 - 2 * bit_parity(jnp.bitwise_and(row_nums, col_nums), 7)).astype(jnp.float32).astype(jnp.bfloat16)

    def mix(group, carry):
        band = pl.ds(pl.multiple_of(group * BAND, BAND), BAND)
        values = []
        for part in range(2):
            value, flip = total[part, band, :], sbuf[part, band, :]
            high = value.astype(jnp.bfloat16)
            low = (value - high.astype(jnp.float32)).astype(jnp.bfloat16)
            both = jnp.concatenate([high * flip, low * flip], axis=0)
            mixed = jnp.dot(walsh, both, preferred_element_type=jnp.float32)
            values += [mixed[:, k * LANES:(k + 1) * LANES] for k in range(4)]
        for stride in (1, 2, 4):
            values = [
                values[k - stride] - values[k] if k & stride else values[k] + values[k + stride]
                for k in range(8)
            ]
        for k in range(8):
            table[pl.ds(pl.multiple_of(k * units + group * BAND, BAND), BAND), :] = values[k]
        return carry

    lax.fori_loop(0, units // BAND, mix, 0, unroll=True)

    lane_nums = lax.broadcasted_iota(jnp.int32, (8, LANES), 1)
    sub_nums = lax.broadcasted_iota(jnp.int32, (8, LANES), 0)

    def pick(d, buffer):
        tile = turn(d)
        found = jnp.zeros((8, LANES), jnp.float32)
        for part in range(2):
            spots_part(d, part, buffer).wait()
            for num in range(4 * part, 4 * part + 4):
                for inner in range(16):
                    for sub in range(8):
                        spot = spots_smem[2 * buffer + part, num % 4, sub * 16 + inner]
                        row = jnp.broadcast_to(table[pl.ds(spot, 1), :], (8, LANES))
                        taken = row if sub == 0 else jnp.where(sub_nums == sub, row, taken)
                    lane = num * 16 + inner
                    value = jnp.sum(taken * weights[tile, lane], axis=1, keepdims=True)
                    found = jnp.where(lane_nums == lane, value, found)

            @pl.when(d < PIECES - 2)
            def _():
                spots_part(d + 2, part, buffer).start()

            if part == 0:
                for num in range(1, PIECES):

                    @pl.when(d == num)
                    def _():
                        ones[num - 1].start()

        terms[d] = found

    def pick_two(num, carry):
        pick(2 * num, 0)
        pick(2 * num + 1, 1)
        return carry

    ones = [
        remote(terms.at[d], first.at[d], send1.at[d], recv1.at[d], across[d]) for d in range(PIECES - 1)
    ]
    lax.fori_loop(0, PIECES // 2, pick_two, 0)
    value = terms[PIECES - 1]
    for d, copy in enumerate(ones):
        copy.wait_recv()
        value = value + first[d]
    second[member] = value
    twos = [
        remote(second.at[member], second.at[member], send2.at[d], recv2.at[d], along[d]) for d in range(SPREAD - 1)
    ]
    for copy in twos:
        copy.start()
    for copy in pending:
        copy.wait_send()
    send_s.wait_send()
    for unit in range(UNITS):
        remote(
            unit_at(1, core, unit), unit_at(3, core, unit), relay_send.at[unit], g_recv.at[3, unit], at_core
        ).wait_send()

    for copy in cross + to_far + hand_on:
        copy.wait_send()
    for d in range(SPREAD - 1):
        source = second.at[mod(member + SPREAD - 1 - d, SPREAD)]
        remote(source, source, send2.at[d], recv2.at[d], along[d]).wait_recv()
    scale = 1.0 / math.sqrt(float(SEQ) * SEQ * 4096)
    for example in range(2):
        parts = [second[8 * hi + 4 * example + num] for hi in range(2) for num in range(4)]
        while len(parts) > 1:
            parts = [parts[k] + parts[k + 1] for k in range(0, len(parts), 2)]
        own[example] = parts[0] * scale
    for example in range(2):
        out[example, piece] = own[example]
    threes = [
        remote(own, out.at[:, piece], send3.at[d], recv3.at[d], across[d]) for d in range(PIECES - 1)
    ]
    for copy in threes:
        copy.start()
    for d in range(PIECES - 1):
        source = out.at[:, sources[d]]
        remote(own, source, send3.at[d], recv3.at[d], across[d]).wait_recv()

    for copy in ones + twos + threes:
        copy.wait_send()


def shards(hidden, out_grad, sign_bits, pick_rows, pick_cols):
    units, features = sign_bits.shape
    tokens = hidden.shape[0]
    part_tokens = out_grad.shape[0]
    dma = pltpu.SemaphoreType.DMA
    tile = (8, LANES)
    hbm, vmem = pl.BlockSpec(memory_space=pltpu.HBM), pl.BlockSpec(memory_space=pltpu.VMEM)
    sums = pl.pallas_call(
        sketch_kernel,
        out_shape=jax.ShapeDtypeStruct((2, PIECES) + tile, jnp.float32),
        in_specs=[hbm] * 5,
        out_specs=vmem,
        scratch_shapes=[
            pltpu.VMEM((2, PIECES * 8, LANES), jnp.int32),
            pltpu.VMEM((4, tokens, units), jnp.bfloat16),
            pltpu.VMEM((4, 2, 2, part_tokens, features), jnp.bfloat16),
            pltpu.VMEM((UNITS, part_tokens // 2, features), jnp.bfloat16),
            pltpu.VMEM((units, features), jnp.int32),
            pltpu.VMEM((2, units, features), jnp.bfloat16),
            pltpu.VMEM((2, units, features), jnp.float32),
            pltpu.VMEM((8 * units, LANES), jnp.float32),
            pltpu.VMEM((PIECES * 2, 4, LANES), jnp.int32),
            pltpu.VMEM((PIECES * 8, LANES), jnp.int32),
            pltpu.VMEM((PIECES, LANES) + tile, jnp.float32),
            pltpu.SMEM((4, 4, LANES), jnp.int32),
            pltpu.VMEM((PIECES,) + tile, jnp.float32),
            pltpu.VMEM((PIECES - 1,) + tile, jnp.float32),
            pltpu.VMEM((SPREAD,) + tile, jnp.float32),
            pltpu.VMEM((2,) + tile, jnp.float32),
            dma((5,)), dma((4,)), dma((2 * CHUNKS,)), dma((2 * CHUNKS,)), dma((3, CHUNKS)), dma((2,)), dma((2,)), dma((2,)), dma((UNITS,)), dma((2, UNITS)),
            dma((UNITS,)), dma((4, UNITS)), dma((4, UNITS)), dma((4, UNITS)), dma, dma,
            dma((PIECES - 1,)), dma((PIECES - 1,)), dma((SPREAD - 1,)), dma((SPREAD - 1,)),
            dma((PIECES - 1,)), dma((PIECES - 1,)),
        ],
        compiler_params=pltpu.CompilerParams(
            collective_id=0, has_side_effects=True, vmem_limit_bytes=62 * 1024 * 1024
        ),
        name="sketch",
    )(hidden, out_grad, sign_bits, pick_rows.reshape(-1, LANES), pick_cols.reshape(-1, LANES))
    return sums.reshape(2, -1)


def solution(mesh):
    placed = (P("narrow", "wide"), P("wide", "narrow"), P("wide", "narrow"), P(), P())
    return jax.shard_map(shards, mesh=mesh, in_specs=placed, out_specs=P(), check_vma=False)
```

```python
import math

import jax
import jax.numpy as jnp
from jax import lax
from jax.experimental import pallas as pl
from jax.experimental.pallas import tpu as pltpu
from jax.sharding import PartitionSpec as P

SEQ = 2048
BAND = 128
LANES = 128
PIECES = 8
SPREAD = 16
UNITS = 4
CHUNKS = 8
BY_Z = (5, 6, 7)
LEAD = 2
MESH = pl.DeviceIdType.MESH


def bit_parity(value, count):
    total = jnp.zeros_like(value)
    for bit_num in range(count):
        total = total + jnp.bitwise_and(jnp.right_shift(value, bit_num), 1)
    return jnp.bitwise_and(total, 1)


def div(value, by):
    return lax.div(value, jnp.int32(by))


def mod(value, by):
    return lax.rem(value, jnp.int32(by))


def place():
    wide, narrow = lax.axis_index("wide"), lax.axis_index("narrow")
    return div(wide, 8), mod(div(wide, 2), 4), mod(wide, 2), div(narrow, 2), mod(narrow, 2)


def device(z_hi, x, core, y, z_lo):
    return (z_hi * 8 + x * 2 + core, y * 2 + z_lo)


def sketch_kernel(
    acts, grads, sign_bits, pick_rows, pick_cols, out,
    picks, hbuf, gbuf, transit, sraw, sbuf, total, table, spots, codes, weights, spots_smem, terms, first, second, own,
    local_sem, spot_sem, hy_send, hz_send, h_recv, init_send, far_send, t_send, t_recv, x_send, relay_send, g_recv,
    core_send, core_recv, s_send, s_recv, send1, recv1, send2, recv2, send3, recv3,
):
    wide, narrow = lax.axis_index("wide"), lax.axis_index("narrow")
    z_hi, x, core, y, z_lo = place()
    units = sraw.shape[0]
    y_bit, upper_y = mod(y, 2), div(y, 2)
    y_pair = y + 1 - 2 * y_bit
    at_y = device(z_hi, x, core, y_pair, z_lo)
    at_z = device(z_hi, x, core, y, 1 - z_lo)
    at_far = device(z_hi, x, core, 3 - y, z_lo)
    at_cross = device(1 - z_hi, x, core, y, 1 - z_lo)
    at_right = device(z_hi, mod(x + 1, 4), core, y, z_lo)
    at_left = device(z_hi, mod(x + 3, 4), core, y, z_lo)
    at_core = device(z_hi, x, 1 - core, y, z_lo)
    holder = upper_y == z_hi
    chunk = acts.shape[0] // CHUNKS

    piece = x * 2 + core
    member = (z_hi * 4 + y) * 2 + z_lo
    ways = ((2, 0), (2, 1), (1, 0), (1, 1), (3, 0), (3, 1), (0, 1))
    pieces = [mod(x + dx, 4) * 2 + mod(core + dc, 2) for dx, dc in ways]
    sources = [mod(x + 4 - dx, 4) * 2 + mod(core + dc, 2) for dx, dc in ways]
    members = [mod(member + d, SPREAD) for d in range(1, SPREAD)]
    across = [(z_hi * 8 + t, narrow) for t in pieces]
    along = [(div(g, 8) * 8 + piece, mod(g, 8)) for g in members]

    barrier = pltpu.get_barrier_semaphore()
    for peer in across + along:
        pl.semaphore_signal(barrier, inc=1, device_id=peer, device_id_type=MESH)
    bits_in = pltpu.make_async_copy(sign_bits, sraw, local_sem.at[1])
    bits_in.start()
    own_h = pltpu.make_async_copy(acts, hbuf.at[0], local_sem.at[0])
    own_h.start()
    picks_in = [
        pltpu.make_async_copy(source, picks.at[num], local_sem.at[3 + num])
        for num, source in enumerate((pick_rows, pick_cols))
    ]
    for copy in picks_in:
        copy.start()
    pl.semaphore_wait(barrier, len(across + along))

    def remote(src, dst, send, recv, target):
        return pltpu.make_async_remote_copy(
            src_ref=src, dst_ref=dst, send_sem=send, recv_sem=recv, device_id=target, device_id_type=MESH
        )

    def arrived(ref, recv):
        remote(ref, ref, s_send, recv, at_core).wait_recv()

    own_g = pltpu.make_async_copy(grads, gbuf.at[0, core, 0], local_sem.at[2])
    few = grads.shape[0] // 2

    def piece_of(ref, unit):
        return ref.at[pl.ds(unit % 2 * few, few)]

    def unit_at(slot, half, unit):
        return gbuf.at[slot, half, unit // 2, pl.ds(unit % 2 * few, few)]

    follower = jnp.logical_not(holder)
    cross = [
        remote(piece_of(grads, unit), transit.at[unit], init_send.at[unit], t_recv.at[unit], at_cross)
        for unit in range(2)
    ]
    to_far = [
        remote(piece_of(grads, unit), unit_at(0, core, 2 + unit), far_send.at[unit], g_recv.at[0, 2 + unit], at_far)
        for unit in range(2)
    ]
    hand_on = [
        remote(transit.at[unit], unit_at(0, core, unit), t_send.at[unit], g_recv.at[0, unit], at_z)
        for unit in range(2)
    ]
    hand_over = [
        remote(transit.at[unit], transit.at[2 + unit], t_send.at[unit], t_recv.at[2 + unit], at_z)
        for unit in range(2)
    ]
    onward = [
        remote(
            transit.at[2 + unit], unit_at(0, core, 2 + unit), far_send.at[unit], g_recv.at[0, 2 + unit], at_far
        )
        for unit in range(2)
    ]
    for copy in cross:
        copy.start()

    @pl.when(holder)
    def _():
        own_g.start()

    @pl.when(follower)
    def _():
        for copy in to_far:
            copy.start()

    pending = []
    by_y = tuple(num for num in range(CHUNKS) if num not in BY_Z)
    def activations(slot, num):
        sends, target = ((hy_send, at_y), (hz_send, at_z))[slot - 1]
        copy = remote(
            acts.at[pl.ds(num * chunk, chunk)], hbuf.at[slot, pl.ds(num * chunk, chunk)],
            sends.at[num], h_recv.at[slot - 1, num], target,
        )
        pending.append(copy)
        return copy

    by_z_pair = [activations(2, num) for num in by_y + BY_Z]
    for copy in by_z_pair[:LEAD]:
        copy.start()
    for num in BY_Z + by_y:
        activations(1, num).start()

    def rows(slot, num):
        return hbuf.at[slot, pl.ds(num * chunk, chunk)]

    def pass_on(slot, num):
        arrived(rows(slot, num), h_recv.at[slot - 1, num])
        sends, target = ((hz_send, at_z), (hy_send, at_y))[slot - 1]
        copy = remote(rows(slot, num), rows(3, num), sends.at[CHUNKS + num], h_recv.at[2, num], target)
        copy.start()
        pending.append(copy)

    def to_sibling(slot, unit):
        block = unit_at(slot, core, unit)
        copy = remote(block, block, core_send.at[slot, unit], core_recv.at[slot, unit], at_core)
        pending.append(copy)
        return copy

    spreads = [
        [
            remote(
                unit_at(0, core, unit), unit_at(side, core, unit), x_send.at[side - 1, unit],
                g_recv.at[side, unit], target,
            )
            for side, target in ((1, at_right), (2, at_left))
        ]
        for unit in range(UNITS)
    ]
    for copies in spreads:
        pending.extend(copies)
    own_siblings = [to_sibling(0, unit) for unit in range(UNITS)]

    def spread(unit):
        for copy in spreads[unit]:
            copy.start()
        own_siblings[unit].start()

    def around(unit):
        for side in (1, 2):
            arrived(unit_at(side, core, unit), g_recv.at[side, unit])
        for side, target in ((1, at_right), (2, at_left)):

            @pl.when(core == side - 1)
            def _():
                remote(
                    unit_at(side, core, unit), unit_at(3, core, unit),
                    relay_send.at[unit], g_recv.at[3, unit], target,
                ).start()

        to_sibling(1, unit).start()
        to_sibling(2, unit).start()

    def opposite(unit):
        arrived(unit_at(3, core, unit), g_recv.at[3, unit])
        to_sibling(3, unit).start()

    def transfer(unit):
        arrived(transit.at[unit], t_recv.at[unit])

        @pl.when(holder)
        def _():
            hand_over[unit].start()

        @pl.when(follower)
        def _():
            hand_on[unit].start()

    def move_on(unit):
        arrived(transit.at[2 + unit], t_recv.at[2 + unit])
        onward[unit].start()

    def own_arrived(unit):
        arrived(unit_at(0, core, unit), g_recv.at[0, unit])

    bits_in.wait()

    def to_sign(group, carry):
        band = pl.ds(pl.multiple_of(group * BAND, BAND), BAND)
        sbuf[0, band, :] = (2 * sraw[band, :] - 1).astype(jnp.float32).astype(jnp.bfloat16)
        return carry

    lax.fori_loop(0, units // BAND, to_sign, 0)

    send_s = remote(sbuf.at[0], sbuf.at[1], s_send, s_recv, at_far)
    for copy in picks_in:
        copy.wait()
    sampled, features = picks[0], picks[1]
    group = jnp.zeros_like(sampled)
    for num in range(1, 16):
        group = group + (sampled >= num * units).astype(jnp.int32)
    block, col = features // 512, features % 512
    upper = bit_parity(jnp.bitwise_and(block, 6), 3)
    spot = (upper * 4 + col // LANES) * units + sampled - group * units
    ahead_of = (lax.broadcasted_iota(jnp.int32, (8, LANES), 1) // 16 + 8 - lax.broadcasted_iota(jnp.int32, (8, LANES), 0)) % 8
    for tile in range(PIECES):
        straight = spot[tile * 8:(tile + 1) * 8]
        turned = straight
        for d in range(1, 8):
            turned = jnp.where(ahead_of == d, pltpu.roll(pltpu.roll(straight, 8 - d, 0), 16 * d, 1), turned)
        for part in range(2):
            spots[tile * 2 + part] = turned[4 * part:4 * part + 4]
    sign = bit_parity(jnp.bitwise_and(group, wide), 4) + bit_parity(jnp.bitwise_and(block, narrow), 3)
    codes[...] = col % LANES + LANES * (sign % 2)

    lane_bits = lax.broadcasted_iota(jnp.int32, (8, LANES), 1) + LANES

    def weigh(first_tile, last_tile):
        def some(num, code):
            for inner in range(16):
                odd = jnp.bitwise_and(jnp.broadcast_to(code[:, inner:inner + 1], (8, LANES)), lane_bits)
                odd = jnp.bitwise_and(lax.population_count(odd), 1)
                weights[num // 8, num % 8 * 16 + inner] = jnp.where(odd == 1, -1.0, 1.0).astype(jnp.float32)
            code = pltpu.roll(code, LANES - 16, 1)
            after = jnp.minimum(num // 8 + 1, PIECES - 1)
            return jnp.where(num % 8 == 7, codes[pl.ds(pl.multiple_of(after * 8, 8), 8), :], code)

        lax.fori_loop(first_tile * 8, last_tile * 8, some, codes[first_tile * 8:(first_tile + 1) * 8, :])

    def turn(d):
        pair = div(d, 2)
        ahead = 2 + 3 * pair + 3 * div(pair, 2) + 2 * div(pair, 3)
        return mod(x + ahead, 4) * 2 + mod(core + d + div(d, 6), 2)

    def spots_part(d, part, buffer):
        tile = turn(d)
        return pltpu.make_async_copy(spots.at[tile * 2 + part], spots_smem.at[2 * buffer + part], spot_sem.at[2 * buffer + part])


    @pl.when(holder)
    def _():
        own_g.wait()
        spread(0)
        spread(1)

    transfer(0)

    @pl.when(holder)
    def _():
        own_arrived(2)
        spread(2)

    weigh(0, 1)
    transfer(1)
    for copy in by_z_pair[LEAD:]:
        copy.start()

    @pl.when(holder)
    def _():
        own_arrived(3)
        spread(3)
        move_on(0)

    @pl.when(follower)
    def _():
        own_arrived(0)
        spread(0)

    for num in BY_Z:
        pass_on(1, num)
    weigh(1, 2)

    @pl.when(holder)
    def _():
        move_on(1)

    @pl.when(follower)
    def _():
        own_arrived(1)
        spread(1)
        own_arrived(2)
        spread(2)

    send_s.start()
    around(0)
    weigh(2, 3)

    @pl.when(follower)
    def _():
        own_arrived(3)
        spread(3)

    around(1)
    weigh(3, 5)
    opposite(0)
    third = (len(by_y) + 2) // 3
    for num in by_y[:third]:
        pass_on(2, num)
    around(2)
    weigh(5, 6)
    opposite(1)
    around(3)
    weigh(6, 8)
    for num in by_y[third:2 * third]:
        pass_on(2, num)
    opposite(2)
    opposite(3)
    for num in by_y[2 * third:]:
        pass_on(2, num)

    total[...] = jnp.zeros_like(total)
    own_h.wait()
    for slot in range(4):
        for unit in range(UNITS):
            arrived(unit_at(slot, 1 - core, unit), core_recv.at[slot, unit])

    depth = acts.shape[0] // 2

    def step(num, carry):
        slot, half = div(num, 2), mod(num, 2)
        for which in (1, 2, 3):
            for one in range(CHUNKS):
                if not ((which == 1 and one in BY_Z) or (which == 2 and one in by_y)):

                    @pl.when(num == 2 * which + one // (CHUNKS // 2))
                    def _():
                        arrived(rows(which, one), h_recv.at[which - 1, one])

        from_y, from_z = mod(slot, 2), div(slot, 2)
        tokens = mod(y_bit + from_y, 2) * 2 + mod(z_lo + from_z, 2)
        ahead = mod(tokens - x + 4, 4)
        source = mod(ahead + div(ahead + 1, 2), 4)
        left = hbuf[slot, pl.ds(pl.multiple_of(half * depth, depth), depth), :]
        for part in range(2):
            total[part] += lax.dot_general(
                left, gbuf[source, half, part], (((0,), (0,)), ((), ())), preferred_element_type=jnp.float32
            )
        return carry

    for part in range(2):
        spots_part(0, part, 0).start()
        spots_part(1, part, 1).start()
    lax.fori_loop(0, 8, step, 0, unroll=2)
    arrived(sbuf.at[1], s_recv)

    row_nums = lax.broadcasted_iota(jnp.int32, (BAND, 2 * BAND), 0)
    col_nums = lax.broadcasted_iota(jnp.int32, (BAND, 2 * BAND), 1)
    walsh = (1 - 2 * bit_parity(jnp.bitwise_and(row_nums, col_nums), 7)).astype(jnp.float32).astype(jnp.bfloat16)

    def mix(group, carry):
        band = pl.ds(pl.multiple_of(group * BAND, BAND), BAND)
        values = []
        for part in range(2):
            value, flip = total[part, band, :], sbuf[part, band, :]
            high = value.astype(jnp.bfloat16)
            low = (value - high.astype(jnp.float32)).astype(jnp.bfloat16)
            both = jnp.concatenate([high * flip, low * flip], axis=0)
            mixed = jnp.dot(walsh, both, preferred_element_type=jnp.float32)
            values += [mixed[:, k * LANES:(k + 1) * LANES] for k in range(4)]
        for stride in (1, 2, 4):
            values = [
                values[k - stride] - values[k] if k & stride else values[k] + values[k + stride]
                for k in range(8)
            ]
        for k in range(8):
            table[pl.ds(pl.multiple_of(k * units + group * BAND, BAND), BAND), :] = values[k]
        return carry

    lax.fori_loop(0, units // BAND, mix, 0, unroll=True)

    lane_nums = lax.broadcasted_iota(jnp.int32, (8, LANES), 1)
    sub_nums = lax.broadcasted_iota(jnp.int32, (8, LANES), 0)

    def pick(d, buffer):
        tile = turn(d)
        found = jnp.zeros((8, LANES), jnp.float32)
        for part in range(2):
            spots_part(d, part, buffer).wait()
            for num in range(4 * part, 4 * part + 4):
                for inner in range(16):
                    for sub in range(8):
                        spot = spots_smem[2 * buffer + part, num % 4, sub * 16 + inner]
                        row = jnp.broadcast_to(table[pl.ds(spot, 1), :], (8, LANES))
                        taken = row if sub == 0 else jnp.where(sub_nums == sub, row, taken)
                    lane = num * 16 + inner
                    value = jnp.sum(taken * weights[tile, lane], axis=1, keepdims=True)
                    found = jnp.where(lane_nums == lane, value, found)

            @pl.when(d < PIECES - 2)
            def _():
                spots_part(d + 2, part, buffer).start()

            if part == 0:
                for num in range(1, PIECES):

                    @pl.when(d == num)
                    def _():
                        ones[num - 1].start()

        terms[d] = found

    def pick_two(num, carry):
        pick(2 * num, 0)
        pick(2 * num + 1, 1)
        return carry

    ones = [
        remote(terms.at[d], first.at[d], send1.at[d], recv1.at[d], across[d]) for d in range(PIECES - 1)
    ]
    lax.fori_loop(0, PIECES // 2, pick_two, 0)
    value = terms[PIECES - 1]
    for d, copy in enumerate(ones):
        copy.wait_recv()
        value = value + first[d]
    second[member] = value
    twos = [
        remote(second.at[member], second.at[member], send2.at[d], recv2.at[d], along[d]) for d in range(SPREAD - 1)
    ]
    for copy in twos:
        copy.start()
    for copy in pending:
        copy.wait_send()
    send_s.wait_send()
    for unit in range(UNITS):
        remote(
            unit_at(1, core, unit), unit_at(3, core, unit), relay_send.at[unit], g_recv.at[3, unit], at_core
        ).wait_send()

    for copy in cross + to_far + hand_on:
        copy.wait_send()
    for d in range(SPREAD - 1):
        source = second.at[mod(member + SPREAD - 1 - d, SPREAD)]
        remote(source, source, send2.at[d], recv2.at[d], along[d]).wait_recv()
    scale = 1.0 / math.sqrt(float(SEQ) * SEQ * 4096)
    for example in range(2):
        parts = [second[8 * hi + 4 * example + num] for hi in range(2) for num in range(4)]
        while len(parts) > 1:
            parts = [parts[k] + parts[k + 1] for k in range(0, len(parts), 2)]
        own[example] = parts[0] * scale
    for example in range(2):
        out[example, piece] = own[example]
    threes = [
        remote(own, out.at[:, piece], send3.at[d], recv3.at[d], across[d]) for d in range(PIECES - 1)
    ]
    for copy in threes:
        copy.start()
    for d in range(PIECES - 1):
        source = out.at[:, sources[d]]
        remote(own, source, send3.at[d], recv3.at[d], across[d]).wait_recv()

    for copy in ones + twos + threes:
        copy.wait_send()


def shards(hidden, out_grad, sign_bits, pick_rows, pick_cols):
    units, features = sign_bits.shape
    tokens = hidden.shape[0]
    part_tokens = out_grad.shape[0]
    dma = pltpu.SemaphoreType.DMA
    tile = (8, LANES)
    hbm, vmem = pl.BlockSpec(memory_space=pltpu.HBM), pl.BlockSpec(memory_space=pltpu.VMEM)
    sums = pl.pallas_call(
        sketch_kernel,
        out_shape=jax.ShapeDtypeStruct((2, PIECES) + tile, jnp.float32),
        in_specs=[hbm] * 5,
        out_specs=vmem,
        scratch_shapes=[
            pltpu.VMEM((2, PIECES * 8, LANES), jnp.int32),
            pltpu.VMEM((4, tokens, units), jnp.bfloat16),
            pltpu.VMEM((4, 2, 2, part_tokens, features), jnp.bfloat16),
            pltpu.VMEM((UNITS, part_tokens // 2, features), jnp.bfloat16),
            pltpu.VMEM((units, features), jnp.int32),
            pltpu.VMEM((2, units, features), jnp.bfloat16),
            pltpu.VMEM((2, units, features), jnp.float32),
            pltpu.VMEM((8 * units, LANES), jnp.float32),
            pltpu.VMEM((PIECES * 2, 4, LANES), jnp.int32),
            pltpu.VMEM((PIECES * 8, LANES), jnp.int32),
            pltpu.VMEM((PIECES, LANES) + tile, jnp.float32),
            pltpu.SMEM((4, 4, LANES), jnp.int32),
            pltpu.VMEM((PIECES,) + tile, jnp.float32),
            pltpu.VMEM((PIECES - 1,) + tile, jnp.float32),
            pltpu.VMEM((SPREAD,) + tile, jnp.float32),
            pltpu.VMEM((2,) + tile, jnp.float32),
            dma((5,)), dma((4,)), dma((2 * CHUNKS,)), dma((2 * CHUNKS,)), dma((3, CHUNKS)), dma((2,)), dma((2,)), dma((2,)), dma((UNITS,)), dma((2, UNITS)),
            dma((UNITS,)), dma((4, UNITS)), dma((4, UNITS)), dma((4, UNITS)), dma, dma,
            dma((PIECES - 1,)), dma((PIECES - 1,)), dma((SPREAD - 1,)), dma((SPREAD - 1,)),
            dma((PIECES - 1,)), dma((PIECES - 1,)),
        ],
        compiler_params=pltpu.CompilerParams(
            collective_id=0, has_side_effects=True, vmem_limit_bytes=62 * 1024 * 1024
        ),
        name="sketch",
    )(hidden, out_grad, sign_bits, pick_rows.reshape(-1, LANES), pick_cols.reshape(-1, LANES))
    return sums.reshape(2, -1)


def solution(mesh):
    placed = (P("narrow", "wide"), P("wide", "narrow"), P("wide", "narrow"), P(), P())
    return jax.shard_map(shards, mesh=mesh, in_specs=placed, out_specs=P(), check_vma=False)
```
